256 devices in a mesh: dp: 32 (over y, x, core), ind: 8 (over z).
Axes of the slice: x: 4, y: 4, z: 8, core: 2. Of those that a mesh axis runs over, the one named last changes fastest.
Arguments:
- inputs: bfloat16 [65536, 256], P('dp'), may hold values from -6 to 6
- targets: bfloat16 [65536], P('dp'), may hold values from -6 to 6
- row_counts: int32 [32], replicated, may hold values from 1 to 2048, 32768 in all
- w_in: bfloat16 [256, 1024], replicated, may hold values from -0.375 to 0.375
- w_mid: bfloat16 [1024, 1024], replicated, may hold values from -0.1875 to 0.1875
- w_out: bfloat16 [1024, 128], replicated, may hold values from -0.1875 to 0.1875
- feat_gain: float32 [128], replicated, may hold values from 0.1 to 1.9
- inducing: bfloat16 [16384, 128], P('ind'), may hold values from -6 to 6
- log_scale: float32 [1], replicated, may hold values from -0.5 to 0.5
- lengthscale: float32 [1], replicated, may hold values from 3.2 to 3.5
- noise_var: float32 [1], replicated, may hold values from 5e-05 to 0.0002
Outputs:
- panel_factor: float32 [16384, 512], P(('ind', 'dp'))
- rhs_next: float32 [16384], P(('ind', 'dp'))
- panel_solution: float32 [512], replicated
- log_det: float32 [1], replicated
The draws below stay inside these ranges and needn't reach their ends.
Inputs may be any that keep to these rules, and one draw needn't show every extreme that they name: The first row_counts[s] samples of shard s are valid; the counts sum to 32768 and one shard has all 2048 slots valid.
All inputs are finite; a program needn't handle non-finite values.
Results may differ from the reference program's by a relative error of at most 0.012.
The reference program's roundings to bfloat16 on the way (of `hidden_one`, `hidden_two`, `embedded`, `panel_kernel` and `kernel_rows`) count: a program that leaves them out, or rounds other values in their place, can miss the bound.
Values may be sent and summed in bfloat16 or wider, within the bound.
No kernel may reach another device: no remote copies, remote signals or barrier semaphores. Data moves between devices by JAX's collectives and lax.ppermute only.
A program may use at most 64 MiB of HBM per device.

```python
import math
import jax
import jax.numpy as jnp
import numpy as np
from jax import lax

DIN = 256
HID = 1024
E = 128
M = 16384
PB = 512
CAP = 2048
TOTAL = 32768
SLOTS = 65536
N_DP = 32


def steps_of(key, shape, cuts, least, top_value):
    gain = 1.0
    for position, shards_of in cuts:
        steps = jax.random.uniform(jax.random.fold_in(jax.random.fold_in(key, 6), position), (shards_of,), jnp.float32, least / len(cuts), top_value / len(cuts))
        gain = gain * jnp.repeat(jnp.exp(steps), shape[position] // shards_of).reshape((-1,) + (1,) * (len(shape) - 1 - position))
    return gain


def length_profile(count, total, limit, skew):
    weights = [(1 << 20) // math.isqrt(grade ** skew) + 1 for grade in range(2, count + 1)]
    surplus, holding = total - limit - (count - 1), [1] * (count - 1)
    while surplus > 0:
        movable = [i for i in range(count - 1) if holding[i] < limit]
        whole, left = sum([weights[i] for i in movable]), surplus
        for i in movable:
            more = min(limit - holding[i], max(1, left * weights[i] // whole), surplus)
            holding[i] = holding[i] + more
            surplus = surplus - more
    return np.array([limit] + holding)


def uneven_parts(key, count, total, most, slope):
    if count == 2:
        one = jax.random.randint(key, (), max(1, total - most), min(most, total - 1) + 1)
        return jnp.stack([one, total - one])
    tallies = jnp.asarray(length_profile(count, total, most, slope), jnp.int32)
    twos = (count - 1) // 2
    source_of, sink = tallies[1:1 + 2 * twos:2], tallies[2:2 + 2 * twos:2]
    margin = jnp.minimum(source_of - 1, most - sink)
    shifted = jax.random.randint(jax.random.fold_in(key, 1), (twos,), 0, 1 << 20) % (margin + 1)
    tallies = tallies.at[1:1 + 2 * twos:2].set(source_of - shifted).at[2:2 + 2 * twos:2].set(sink + shifted)
    return tallies[jax.random.permutation(jax.random.fold_in(key, 2), count)]


def bell_draw(own_key, dims, spread, most, cuts=(), kind=jnp.bfloat16):
    loudness = steps_of(own_key, dims, cuts, -0.22, 0.18) if cuts else 1.0
    array = jax.random.normal(own_key, dims, jnp.float32) * spread * loudness
    return jnp.minimum(jnp.maximum(array, -most), most).astype(kind)


def setup_inputs(seed: int = 0) -> dict:
    streams_of = jax.random.split(jax.random.key(seed), 12)
    return {
        "inputs": bell_draw(streams_of[0], (SLOTS, DIN), 1.0, 6.0, ((0, 32),)),
        "targets": bell_draw(streams_of[1], (SLOTS,), 1.0, 6.0, ((0, 32),)),
        "row_counts": uneven_parts(streams_of[2], N_DP, TOTAL, CAP, 2).astype(jnp.int32),
        "w_in": bell_draw(streams_of[3], (DIN, HID), DIN ** -0.5, 0.375),
        "w_mid": bell_draw(streams_of[4], (HID, HID), HID ** -0.5, 0.1875),
        "w_out": bell_draw(streams_of[5], (HID, E), HID ** -0.5, 0.1875),
        "feat_gain": jnp.clip(1.0 + 0.18 * jax.random.normal(streams_of[6], (E,), jnp.float32), 0.1, 1.9),
        "inducing": bell_draw(streams_of[7], (M, E), 1.0, 6.0, ((0, 8),)),
        "log_scale": jnp.clip(jax.random.uniform(streams_of[8], (1,), jnp.float32, -0.5, 0.5), -0.5, 0.5),
        "lengthscale": jnp.clip(jax.random.uniform(streams_of[9], (1,), jnp.float32, 3.2, 3.5), 3.2, 3.5),
        "noise_var": jnp.clip(jnp.exp(jax.random.uniform(streams_of[10], (1,), jnp.float32, math.log(4.999999873689376e-05), math.log(0.0002))), 4.999999873689376e-05, 0.0002),
    }


JITTER = 0.0001

def embed(inputs, w_in, w_mid, w_out, feat_gain):
    hidden_one = jax.nn.gelu(jnp.dot(inputs.astype(jnp.float32), w_in.astype(jnp.float32), preferred_element_type=jnp.float32)).astype(jnp.bfloat16)
    hidden_two = jax.nn.gelu(jnp.dot(hidden_one.astype(jnp.float32), w_mid.astype(jnp.float32), preferred_element_type=jnp.float32)).astype(jnp.bfloat16)
    projected = jnp.dot(hidden_two.astype(jnp.float32), w_out.astype(jnp.float32), preferred_element_type=jnp.float32)
    scaled = projected * lax.rsqrt(lax.optimization_barrier(jnp.mean(projected * projected, axis=-1, keepdims=True)) + 1e-06) * feat_gain
    return scaled.astype(jnp.bfloat16)

def exponent(points, others, scale_log, inverse_sq):
    point_sq = lax.optimization_barrier(jnp.sum(jnp.square(points.astype(jnp.float32)), axis=1))
    other_sq = lax.optimization_barrier(jnp.sum(jnp.square(others.astype(jnp.float32)), axis=1))
    cross_term = jnp.dot(points.astype(jnp.float32), others.T.astype(jnp.float32), preferred_element_type=jnp.float32)
    return scale_log - 0.5 * inverse_sq * (point_sq[:, None] + other_sq[None, :]) + inverse_sq * cross_term

def reference(inputs, targets, row_counts, w_in, w_mid, w_out, feat_gain, inducing, log_scale, lengthscale, noise_var):
    shards = row_counts.shape[0]
    capacity = inputs.shape[0] // shards
    embedded = embed(inputs, w_in, w_mid, w_out, feat_gain)
    row_index = jnp.arange(capacity, dtype=jnp.int32)
    valid_rows = (row_index[None, :] < row_counts[:, None]).reshape(-1)
    scale_log = log_scale[0]
    inverse_sq = 1.0 / (lengthscale[0] * lengthscale[0])
    variance = noise_var[0]
    panel_points = inducing[:PB]
    panel_kernel = jnp.where(valid_rows[None, :], jnp.exp(exponent(panel_points, embedded, scale_log, inverse_sq)), 0.0).astype(jnp.bfloat16)
    target_used = jnp.where(valid_rows, targets, jnp.zeros_like(targets))
    block_size = min(512, M)
    grouped = inducing.reshape(M // block_size, block_size, inducing.shape[1])

    def gram_block(points):
        kernel_rows = jnp.exp(exponent(points, embedded, scale_log, inverse_sq)).astype(jnp.bfloat16)
        return (jnp.dot(kernel_rows.astype(jnp.float32), panel_kernel.T.astype(jnp.float32), preferred_element_type=jnp.float32), jnp.dot(kernel_rows.astype(jnp.float32), target_used.astype(jnp.float32), preferred_element_type=jnp.float32))
    gram_rows, cross_rows = lax.map(gram_block, grouped)
    gram_rows = gram_rows.reshape(M, PB)
    cross_rows = cross_rows.reshape(M)
    diagonal_mask = jnp.arange(M, dtype=jnp.int32)[:, None] == jnp.arange(PB, dtype=jnp.int32)[None, :]
    kernel_mm = jnp.exp(exponent(inducing, panel_points, scale_log, inverse_sq)) + jnp.where(diagonal_mask, JITTER, 0.0)
    system_rows = kernel_mm + gram_rows / variance
    right_side = cross_rows / variance
    factor_top = jnp.linalg.cholesky(system_rows[:PB])
    log_det = 2.0 * jnp.sum(jnp.log(jnp.diagonal(factor_top)))
    panel_solution = lax.linalg.triangular_solve(factor_top, right_side[:PB, None], left_side=True, lower=True)[:, 0]
    panel_factor = lax.linalg.triangular_solve(factor_top, system_rows, left_side=False, lower=True, transpose_a=True)
    rhs_next = right_side - jnp.dot(panel_factor, panel_solution, precision=lax.Precision.HIGHEST)
    return (panel_factor, rhs_next, panel_solution, log_det.reshape(1))
```

```python
import functools
import jax
import jax.numpy as jnp
from jax import lax
from jax.experimental import pallas as pl
from jax.experimental.pallas import tpu as pltpu
from jax.sharding import PartitionSpec as P

PB = 512
JITTER = 0.0001
LOG2E = 1.4426950408889634
LN2 = 0.6931471805599453
MASKED = -1.0e6
F32, BF16 = jnp.float32, jnp.bfloat16
HI = lax.Precision.HIGHEST
NT = (((1,), (1,)), ((), ()))
TN = (((0,), (0,)), ((), ()))


def vmem(limit=60 << 20):
    return pltpu.CompilerParams(vmem_limit_bytes=limit)


def widen(points, half, first):
    rows = points.shape[0]
    high = half.astype(BF16)
    rest = half - high.astype(F32)
    mid = rest.astype(BF16)
    low = (rest - mid.astype(F32)).astype(BF16)
    lane = lax.broadcasted_iota(jnp.int32, (rows, 128), 1)
    at = 0 if first else 3
    one = 3 if first else 0
    tail = jnp.where((lane >= one) & (lane < one + 3), 1.0, 0.0)
    tail = jnp.where(lane == at, high.astype(F32), tail)
    tail = jnp.where(lane == at + 1, mid.astype(F32), tail)
    tail = jnp.where(lane == at + 2, low.astype(F32), tail)
    return jnp.concatenate([points, tail.astype(BF16)], axis=1)


def half_norm(points):
    wide = points.astype(F32)
    return -0.5 * jnp.sum(wide * wide, axis=1, keepdims=True)


def gelu(x):
    inner = x * (0.7978845608028654 + 0.035677408136300125 * (x * x))
    half = 0.5 * x
    return half + half * jnp.tanh(inner)


def embed_kernel(count_ref, x_ref, w1_ref, w2_ref, w3_ref, gain_ref, out_ref):
    rows = x_ref.shape[0]
    one = gelu(jnp.dot(x_ref[...], w1_ref[...], preferred_element_type=F32)).astype(BF16)
    two = gelu(jnp.dot(one, w2_ref[...], preferred_element_type=F32)).astype(BF16)
    proj = jnp.dot(two, w3_ref[...], preferred_element_type=F32)
    mean = jnp.mean(proj * proj, axis=1, keepdims=True)
    points = (proj * lax.rsqrt(mean + 1e-06) * gain_ref[...]).astype(BF16)
    index = pl.program_id(0) * rows + lax.broadcasted_iota(jnp.int32, (rows, 1), 0)
    half = jnp.where(index < count_ref[0], half_norm(points), MASKED)
    out_ref[...] = widen(points, half, False)


def embed(count, inputs, w_in, w_mid, w_out, gain, tile=512):
    slots = inputs.shape[0]
    whole = lambda a: pl.BlockSpec(a.shape, lambda i: (0, 0), pipeline_mode=pl.Buffered(1))
    return pl.pallas_call(
        embed_kernel,
        out_shape=jax.ShapeDtypeStruct((slots, 256), BF16),
        grid=(slots // tile,),
        in_specs=[
            pl.BlockSpec(memory_space=pltpu.SMEM),
            pl.BlockSpec((tile, inputs.shape[1]), lambda i: (i, 0)),
            whole(w_in),
            whole(w_mid),
            whole(w_out),
            whole(gain),
        ],
        out_specs=pl.BlockSpec((tile, 256), lambda i: (i, 0)),
        compiler_params=vmem(),
        cost_estimate=pl.CostEstimate(flops=6 * 10**9, bytes_accessed=5 << 20, transcendentals=4 << 20),
        name="embed",
    )(count, inputs, w_in, w_mid, w_out, gain)


def panel_kernel(scale_ref, samples_ref, panel_ref, chunk_ref, tcol_ref, trow_ref, pt_ref, top_ref):
    step = pl.program_id(0)
    i2, offset = scale_ref[0], scale_ref[1]
    samples = samples_ref[...]
    panel = widen(panel_ref[...], half_norm(panel_ref[...]) + offset, True)
    chunk = widen(chunk_ref[...], half_norm(chunk_ref[...]) + offset, True)
    kern = jnp.exp2(i2 * lax.dot_general(samples, panel, NT, preferred_element_type=F32)).astype(BF16)
    part = jnp.exp2(i2 * lax.dot_general(chunk, samples, NT, preferred_element_type=F32)).astype(BF16)
    left = jnp.concatenate([part, trow_ref[...]], axis=0)
    lane = lax.broadcasted_iota(jnp.int32, (samples.shape[0], 128), 1)
    column = jnp.where(lane == 0, tcol_ref[...].astype(F32), 0.0).astype(BF16)
    pt_ref[:, :PB] = kern
    pt_ref[:, PB:] = column
    sums = jnp.dot(left, kern, preferred_element_type=F32)

    @pl.when(step == 0)
    def _():
        top_ref[...] = sums

    @pl.when(step > 0)
    def _():
        top_ref[...] += sums


def panel_top(scales, samples, panel, chunk, tcol, trow, tile=512):
    slots = samples.shape[0]
    rows = chunk.shape[0] + trow.shape[0]
    fixed = lambda a: pl.BlockSpec(a.shape, lambda i: (0, 0))
    return pl.pallas_call(
        panel_kernel,
        out_shape=(jax.ShapeDtypeStruct((slots, PB + 128), BF16), jax.ShapeDtypeStruct((rows, PB), F32)),
        grid=(slots // tile,),
        in_specs=[
            pl.BlockSpec(memory_space=pltpu.SMEM),
            pl.BlockSpec((tile, 256), lambda i: (i, 0)),
            fixed(panel),
            fixed(chunk),
            pl.BlockSpec((tile, 1), lambda i: (i, 0)),
            pl.BlockSpec((trow.shape[0], tile), lambda i: (0, i)),
        ],
        out_specs=(pl.BlockSpec((tile, PB + 128), lambda i: (i, 0)), pl.BlockSpec((rows, PB), lambda i: (0, 0))),
        compiler_params=vmem(),
        cost_estimate=pl.CostEstimate(flops=10**9, bytes_accessed=5 << 20, transcendentals=1 << 20),
        name="panel",
    )(scales, samples, panel, chunk, tcol, trow)


def gram_kernel(scale_ref, points_ref, samples_ref, pt_ref, out_ref):
    i2, offset = scale_ref[0], scale_ref[1]
    rows = points_ref.shape[0]
    points = widen(points_ref[...], half_norm(points_ref[...]) + offset, True)
    kern = jnp.exp2(
        i2 * lax.dot_general(points, samples_ref[...], NT, preferred_element_type=F32)
    ).astype(BF16)
    sums = jnp.dot(kern, pt_ref[...], preferred_element_type=F32)
    crossed = sums[:, PB:].T
    for b in range(rows // 64):
        out_ref[b, :64, :] = sums[b * 64 : b * 64 + 64, :PB]
        out_ref[b, 64:, :] = jnp.concatenate(
            [crossed[:8, b * 64 : b * 64 + 64], jnp.zeros((8, PB - 64), F32)], axis=1
        )


def gram(scales, points, samples, pt, tile=256):
    total = points.shape[0]
    whole = lambda a: pl.BlockSpec(a.shape, lambda i: (0, 0), pipeline_mode=pl.Buffered(1))
    return pl.pallas_call(
        gram_kernel,
        out_shape=jax.ShapeDtypeStruct((total // 64, 72, PB), F32),
        grid=(total // tile,),
        in_specs=[
            pl.BlockSpec(memory_space=pltpu.SMEM),
            pl.BlockSpec((tile, 128), lambda i: (i, 0)),
            whole(samples),
            whole(pt),
        ],
        out_specs=pl.BlockSpec((tile // 64, 72, PB), lambda i: (i, 0, 0)),
        compiler_params=vmem(),
        cost_estimate=pl.CostEstimate(flops=8 * 10**9, bytes_accessed=9 << 20, transcendentals=4 << 20),
        name="gram",
    )(scales, points, samples, pt)


def invert_block(block, store, note):
    groups = [block[8 * v : 8 * v + 8, :] for v in range(16)]
    lane = lax.broadcasted_iota(jnp.int32, (8, 128), 1)
    pivots = jnp.ones((8, 128), F32)
    spread = lambda a: jnp.broadcast_to(a, (8, 128))
    for g in range(32):
        j = 4 * g
        v, s = j // 8, j % 8
        inside = (lane >= j) & (lane < j + 4)
        raw = [spread(groups[v][s + a : s + a + 1, :]) for a in range(4)]
        p = [[spread(raw[a][:, j + b : j + b + 1]) for b in range(a + 1)] for a in range(4)]
        live = [u for u in range(v, 16) if not (u == v and s == 4)]
        cols = {u: [spread(groups[u][:, j + b : j + b + 1]) for b in range(4)] for u in live}
        d0 = p[0][0]
        i0 = 1.0 / d0
        l10, l20, l30 = p[1][0] * i0, p[2][0] * i0, p[3][0] * i0
        d1 = p[1][1] - l10 * p[1][0]
        i1 = 1.0 / d1
        q21, q31 = p[2][1] - l20 * p[1][0], p[3][1] - l30 * p[1][0]
        l21, l31 = q21 * i1, q31 * i1
        d2 = p[2][2] - l20 * p[2][0] - l21 * q21
        i2 = 1.0 / d2
        q32 = p[3][2] - l30 * p[2][0] - l31 * q21
        l32 = q32 * i2
        d3 = p[3][3] - l30 * p[3][0] - l31 * q31 - l32 * q32
        i3 = 1.0 / d3
        r = [
            jnp.where(inside, jnp.where(lane == j + a, 1.0, 0.0), raw[a]) for a in range(4)
        ]
        r[1] = r[1] - l10 * r[0]
        r[2] = r[2] - l20 * r[0] - l21 * r[1]
        r[3] = r[3] - l30 * r[0] - l31 * r[1] - l32 * r[2]
        for a, d in enumerate((d0, d1, d2, d3)):
            store(j + a, r[a] * lax.rsqrt(d))
            pivots = jnp.where(lane == j + a, d, pivots)
        q3 = r[3] * i3
        q2 = r[2] * i2 - l32 * q3
        q1 = r[1] * i1 - l21 * q2 - l31 * q3
        q0 = r[0] * i0 - l10 * q1 - l20 * q2 - l30 * q3
        for u in live:
            c = cols[u]
            base = jnp.where(inside, 0.0, groups[u])
            groups[u] = base - (c[0] * q0 + c[1] * q1) - (c[2] * q2 + c[3] * q3)
    return pivots


def factor_kernel(scale_ref, panel_ref, top_ref, inverse_ref, log_ref, work, piece):
    i2, offset, over, jit = scale_ref[0], scale_ref[1], scale_ref[2], scale_ref[3]
    half = half_norm(panel_ref[...])
    left = widen(panel_ref[...], half + offset, True)
    right = widen(panel_ref[...], half, False)
    kern = jnp.exp2(i2 * lax.dot_general(left, right, NT, preferred_element_type=F32))
    row = lax.broadcasted_iota(jnp.int32, (PB, PB), 0)
    col = lax.broadcasted_iota(jnp.int32, (PB, PB), 1)
    work[...] = kern + jnp.where(row == col, jit, 0.0) + top_ref[...] * over
    total = jnp.zeros((8, 128), F32)
    lane = lax.broadcasted_iota(jnp.int32, (128, 128), 1)

    def store(r, line):
        piece[r : r + 1, :] = line[:1, :]

    for k in range(PB // 128):
        lo, hi = 128 * k, 128 * k + 128
        lower = lax.broadcasted_iota(jnp.int32, (128, 128), 0) >= lane
        pivots = invert_block(work[lo:hi, lo:hi], store, None)
        total = total + jnp.log(pivots)
        t = jnp.where(lower, piece[...], 0.0)
        rest = jnp.dot(t, work[lo:hi, :], preferred_element_type=F32, precision=HI)
        parts = [rest[:, :lo]] * (lo > 0) + [t] + [rest[:, hi:]] * (hi < PB)
        u = jnp.concatenate(parts, axis=1)
        inverse_ref[lo:hi, :] = jnp.where(
            lax.broadcasted_iota(jnp.int32, (128, PB), 1) < hi, u, 0.0
        )
        if hi < PB:
            away = lax.dot_general(u[:, hi:], u, TN, preferred_element_type=F32, precision=HI)
            column = lax.broadcasted_iota(jnp.int32, (PB - hi, PB), 1)
            kept = jnp.where((column >= lo) & (column < hi), 0.0, work[hi:, :])
            work[hi:, :] = kept - away
    log_ref[...] = jnp.broadcast_to(jnp.sum(total[:1, :], axis=1, keepdims=True), (8, 128))


def factor(scales, panel, top):
    return pl.pallas_call(
        factor_kernel,
        out_shape=(jax.ShapeDtypeStruct((PB, PB), F32), jax.ShapeDtypeStruct((8, 128), F32)),
        in_specs=[
            pl.BlockSpec(memory_space=pltpu.SMEM),
            pl.BlockSpec(memory_space=pltpu.VMEM),
            pl.BlockSpec(memory_space=pltpu.VMEM),
        ],
        out_specs=(pl.BlockSpec(memory_space=pltpu.VMEM), pl.BlockSpec(memory_space=pltpu.VMEM)),
        scratch_shapes=[pltpu.VMEM((PB, PB), F32), pltpu.VMEM((128, 128), F32)],
        compiler_params=vmem(),
        cost_estimate=pl.CostEstimate(flops=20 * 10**9, bytes_accessed=4 << 20, transcendentals=1 << 20),
        name="factor",
    )(scales, panel, top)


def finish_kernel(place_ref, scale_ref, own_ref, panel_ref, sums_ref, right_ref, inverse_ref, pf_ref, rhs_ref, sol_ref):
    i2, offset, over, jit = scale_ref[0], scale_ref[1], scale_ref[2], scale_ref[3]
    rows = own_ref.shape[0]
    left = widen(own_ref[...], half_norm(own_ref[...]) + offset, True)
    right = widen(panel_ref[...], half_norm(panel_ref[...]), False)
    kern = jnp.exp2(i2 * lax.dot_general(left, right, NT, preferred_element_type=F32))
    row = place_ref[0] + lax.broadcasted_iota(jnp.int32, (rows, PB), 0)
    col = lax.broadcasted_iota(jnp.int32, (rows, PB), 1)
    system = kern + jnp.where(row == col, jit, 0.0) + sums_ref[:rows, :] * over
    both = jnp.concatenate([system, right_ref[...] * over], axis=0)
    solved = lax.dot_general(both, inverse_ref[...], NT, preferred_element_type=F32, precision=HI)
    pf = solved[:rows, :]
    sol = solved[rows:, :]
    pf_ref[...] = pf
    sol_ref[...] = sol
    back = lax.dot_general(sol, pf, NT, preferred_element_type=F32, precision=HI)
    rhs_ref[...] = sums_ref[rows:, :rows] * over - back


def finish(place, scales, own, panel, sums, right, inverse):
    rows = own.shape[0]
    smem = pl.BlockSpec(memory_space=pltpu.SMEM)
    full = pl.BlockSpec(memory_space=pltpu.VMEM)
    return pl.pallas_call(
        finish_kernel,
        out_shape=(
            jax.ShapeDtypeStruct((rows, PB), F32),
            jax.ShapeDtypeStruct((8, rows), F32),
            jax.ShapeDtypeStruct((8, PB), F32),
        ),
        in_specs=[smem, smem] + [full] * 5,
        out_specs=(full, full, full),
        compiler_params=vmem(),
        cost_estimate=pl.CostEstimate(flops=10**9, bytes_accessed=2 << 20, transcendentals=1 << 16),
        name="finish",
    )(place, scales, own, panel, sums, right, inverse)


SHARDS, LAYERS = 32, 8


def moved(x, axis, size, to):
    return lax.ppermute(x, axis, [(i, to(i)) for i in range(size)])


def along_x(i, k):
    return (i // 8) * 8 + (i + 2 * k) % 8


def along_y(i, k):
    return (i + 8 * k) % SHARDS


def sum_over(x, step):
    return x + sum(moved(x, "dp", SHARDS, functools.partial(step, k=k)) for k in (1, 2, 3))


def top_everywhere(top, core):
    rows = top.shape[1]
    kept = lax.dynamic_index_in_dim(top, core, 0, False)
    sent = lax.dynamic_index_in_dim(top, 1 - core, 0, False)
    half = kept + moved(sent, "dp", SHARDS, lambda i: i ^ 1)
    half = sum_over(half, along_x)
    half = sum_over(half, along_y)
    layer = lax.axis_index("ind")
    parts = jnp.zeros((LAYERS, rows, 256), F32)
    ahead = behind = half
    parts = lax.dynamic_update_index_in_dim(parts, half, layer, 0)
    for k in range(1, 5):
        ahead = moved(ahead, "ind", LAYERS, lambda i: (i + 1) % LAYERS)
        parts = lax.dynamic_update_index_in_dim(parts, ahead, (layer - k) % LAYERS, 0)
        if k < 4:
            behind = moved(behind, "ind", LAYERS, lambda i: (i - 1) % LAYERS)
            parts = lax.dynamic_update_index_in_dim(parts, behind, (layer + k) % LAYERS, 0)
    other = moved(parts, "dp", SHARDS, lambda i: i ^ 1)
    left = jnp.where(core == 0, parts, other)
    right = jnp.where(core == 0, other, parts)
    return jnp.concatenate([left, right], axis=2)


def body(
    inputs, targets, row_counts, w_in, w_mid, w_out, feat_gain, inducing, log_scale, lengthscale, noise_var
):
    shard = lax.axis_index("dp")
    layer = lax.axis_index("ind")
    core = shard % 2
    slots = inputs.shape[0]
    inv_sq = 1.0 / (lengthscale[0] * lengthscale[0])
    scales = jnp.stack(
        [inv_sq * LOG2E, log_scale[0] / inv_sq, 1.0 / noise_var[0], jnp.asarray(JITTER, F32)]
    )
    first = inducing[:PB]
    panel = first
    for k in range(1, LAYERS):
        got = lax.ppermute(first, "ind", [(0, k)])
        panel = jnp.where(layer == k, got, panel)
    count = lax.dynamic_slice_in_dim(row_counts, shard, 1, 0)
    samples = embed(count, inputs, w_in, w_mid, w_out, feat_gain.reshape(1, -1))
    chunk = lax.dynamic_slice_in_dim(panel, layer * 64, 64, 0)
    trow = jnp.broadcast_to(targets.reshape(1, slots), (8, slots))
    pt, top = panel_top(scales, samples, panel, chunk, targets.reshape(slots, 1), trow)
    rows = top.shape[0]
    whole = top_everywhere(jnp.stack([top[:, :256], top[:, 256:]]), core)
    sums = gram(scales, inducing, samples, pt)
    own = lax.psum_scatter(sums, "dp", scatter_dimension=0, tiled=True)[0]
    system_top = whole[:, :64].reshape(PB, PB)
    right_top = whole[0, 64:]
    inverse, logs = factor(scales, panel, system_top)
    own_rows = inducing.shape[0] // SHARDS
    points = lax.dynamic_slice_in_dim(inducing, shard * own_rows, own_rows, 0)
    place = (layer * inducing.shape[0] + shard * own_rows).reshape(1).astype(jnp.int32)
    pf, rhs, sol = finish(place, scales, points, panel, own, right_top, inverse)
    return pf, rhs[0], sol[0], logs[0, :1]


def solution(mesh):
    return jax.shard_map(
        body,
        mesh=mesh,
        in_specs=(P("dp", None), P("dp"), P(), P(), P(), P(), P(), P("ind", None), P(), P(), P()),
        out_specs=(P(("ind", "dp"), None), P(("ind", "dp")), P(), P()),
        check_vma=False,
    )
```

```python
import functools
import jax
import jax.numpy as jnp
from jax import lax
from jax.experimental import pallas as pl
from jax.experimental.pallas import tpu as pltpu
from jax.sharding import PartitionSpec as P

PB = 512
JITTER = 0.0001
SHARDS, LAYERS = 32, 8
LOG2E = 1.4426950408889634
MASKED = -1.0e6
F32, BF16 = jnp.float32, jnp.bfloat16
HI = lax.Precision.HIGHEST
NT = (((1,), (1,)), ((), ()))
TN = (((0,), (0,)), ((), ()))


def vmem(limit=60 << 20):
    return pltpu.CompilerParams(vmem_limit_bytes=limit)


def widen(points, half, first):
    rows = points.shape[0]
    high = half.astype(BF16)
    rest = half - high.astype(F32)
    mid = rest.astype(BF16)
    low = (rest - mid.astype(F32)).astype(BF16)
    lane = lax.broadcasted_iota(jnp.int32, (rows, 128), 1)
    at = 0 if first else 3
    one = 3 if first else 0
    tail = jnp.where((lane >= one) & (lane < one + 3), 1.0, 0.0)
    tail = jnp.where(lane == at, high.astype(F32), tail)
    tail = jnp.where(lane == at + 1, mid.astype(F32), tail)
    tail = jnp.where(lane == at + 2, low.astype(F32), tail)
    return jnp.concatenate([points, tail.astype(BF16)], axis=1)


def half_norm(points):
    wide = points.astype(F32)
    return -0.5 * jnp.sum(wide * wide, axis=1, keepdims=True)


def gelu(x):
    inner = x * (0.7978845608028654 + 0.035677408136300125 * (x * x))
    half = 0.5 * x
    return half + half * jnp.tanh(inner)


def embed_kernel(base, ids_ref, counts_ref, x_ref, w1_ref, w2_ref, w3_ref, gain_ref, *rest):
    out_ref = rest[-1]
    rows = x_ref.shape[0]
    one = gelu(jnp.dot(x_ref[...], w1_ref[...], preferred_element_type=F32)).astype(BF16)
    two = gelu(jnp.dot(one, w2_ref[...], preferred_element_type=F32)).astype(BF16)
    proj = jnp.dot(two, w3_ref[...], preferred_element_type=F32)
    mean = jnp.mean(proj * proj, axis=1, keepdims=True)
    points = (proj * lax.rsqrt(mean + 1e-06) * gain_ref[...]).astype(BF16)
    index = (base + pl.program_id(0)) * rows + lax.broadcasted_iota(jnp.int32, (rows, 1), 0)
    half = jnp.where(index < counts_ref[ids_ref[0]], half_norm(points), MASKED)
    out_ref[...] = widen(points, half, False)


def embed(base, steps, ids, counts, inputs, w_in, w_mid, w_out, gain, before=None, tile=512):
    slots = inputs.shape[0]
    whole = lambda a: pl.BlockSpec(a.shape, lambda i: (0, 0), pipeline_mode=pl.Buffered(1))
    smem = pl.BlockSpec(memory_space=pltpu.SMEM)
    more = () if before is None else (before,)
    return pl.pallas_call(
        functools.partial(embed_kernel, base),
        out_shape=jax.ShapeDtypeStruct((slots, 256), BF16),
        grid=(steps,),
        in_specs=[
            smem,
            smem,
            pl.BlockSpec((tile, inputs.shape[1]), lambda i: (i + base, 0)),
            whole(w_in),
            whole(w_mid),
            whole(w_out),
            whole(gain),
        ]
        + [pl.BlockSpec(memory_space=pl.ANY)] * len(more),
        out_specs=pl.BlockSpec((tile, 256), lambda i: (i + base, 0)),
        input_output_aliases={7: 0} if more else {},
        compiler_params=vmem(),
        cost_estimate=pl.CostEstimate(
            flops=steps * 15 * 10**8, bytes_accessed=4 << 20, transcendentals=steps << 20
        ),
        name="embed",
    )(ids, counts, inputs, w_in, w_mid, w_out, gain, *more)


def panel_kernel(ids_ref, scale_ref, samples_ref, panel_ref, t_ref, pt_ref, top_ref):
    step = pl.program_id(0)
    i2, offset = scale_ref[0], scale_ref[1]
    samples = samples_ref[...]
    panel = widen(panel_ref[...], half_norm(panel_ref[...]) + offset, True)
    mine = panel_ref[pl.ds(pl.multiple_of(ids_ref[1] * 64, 64), 64), :]
    chunk = widen(mine, half_norm(mine) + offset, True)
    kern = jnp.exp2(i2 * lax.dot_general(samples, panel, NT, preferred_element_type=F32)).astype(BF16)
    part = jnp.exp2(i2 * lax.dot_general(chunk, samples, NT, preferred_element_type=F32)).astype(BF16)
    targets = jnp.broadcast_to(t_ref[...], (8, t_ref.shape[1])).astype(BF16)
    left = jnp.concatenate([part, targets], axis=0)
    pt_ref[...] = kern
    sums = jnp.dot(left, kern, preferred_element_type=F32)

    @pl.when(step == 0)
    def _():
        for h in range(2):
            top_ref[h, :, :] = sums[:, 256 * h : 256 * h + 256]

    @pl.when(step > 0)
    def _():
        for h in range(2):
            top_ref[h, :, :] += sums[:, 256 * h : 256 * h + 256]


def panel_top(ids, scales, samples, panel, targets, tile=512):
    slots = samples.shape[0]
    smem = pl.BlockSpec(memory_space=pltpu.SMEM)
    return pl.pallas_call(
        panel_kernel,
        out_shape=(jax.ShapeDtypeStruct((slots, PB), BF16), jax.ShapeDtypeStruct((2, 72, 256), F32)),
        grid=(slots // tile,),
        in_specs=[
            smem,
            smem,
            pl.BlockSpec((tile, 256), lambda i: (i, 0)),
            pl.BlockSpec(panel.shape, lambda i: (0, 0)),
            pl.BlockSpec((1, tile), lambda i: (0, i)),
        ],
        out_specs=(
            pl.BlockSpec((tile, PB), lambda i: (i, 0)),
            pl.BlockSpec((2, 72, 256), lambda i: (0, 0, 0)),
        ),
        compiler_params=vmem(),
        cost_estimate=pl.CostEstimate(flops=15 * 10**8, bytes_accessed=4 << 20, transcendentals=1 << 20),
        name="panel",
    )(ids, scales, samples, panel, targets)


def gram_kernel(order_ref, scale_ref, *refs):
    points_refs, (samples_ref, pt_ref, t_ref, out_ref) = refs[:4], refs[4:]
    i2, offset = scale_ref[0], scale_ref[1]
    raw = jnp.concatenate([p[...] for p in points_refs], axis=0)
    points = widen(raw, half_norm(raw) + offset, True)
    kern = jnp.exp2(
        i2 * lax.dot_general(points, samples_ref[...], NT, preferred_element_type=F32)
    ).astype(BF16)
    crossed = jnp.sum(kern.astype(F32) * t_ref[...], axis=1, keepdims=True)
    crossed = jnp.broadcast_to(crossed, (256, 128)).T
    sums = jnp.dot(kern, pt_ref[...], preferred_element_type=F32)
    for b in range(4):
        out_ref[b, :64, :] = sums[b * 64 : b * 64 + 64, :]
        out_ref[b, 64:, :] = jnp.concatenate(
            [crossed[:8, b * 64 : b * 64 + 64], jnp.zeros((8, PB - 64), F32)], axis=1
        )


def gram(order, scales, points, samples, pt, targets):
    count = order.shape[0]
    whole = lambda a: pl.BlockSpec(a.shape, lambda i, o: (0, 0), pipeline_mode=pl.Buffered(1))
    block = lambda q: pl.BlockSpec((64, 128), lambda i, o: (o[4 * i + q], 0))
    return pl.pallas_call(
        gram_kernel,
        out_shape=jax.ShapeDtypeStruct((count, 72, PB), F32),
        grid_spec=pltpu.PrefetchScalarGridSpec(
            num_scalar_prefetch=1,
            grid=(count // 4,),
            in_specs=[pl.BlockSpec(memory_space=pltpu.SMEM)]
            + [block(q) for q in range(4)]
            + [whole(samples), whole(pt), whole(targets)],
            out_specs=pl.BlockSpec((4, 72, PB), lambda i, o: (i, 0, 0)),
        ),
        compiler_params=vmem(),
        cost_estimate=pl.CostEstimate(flops=count * 2 * 10**8, bytes_accessed=6 << 20, transcendentals=2 << 20),
        name="gram",
    )(order, scales, points, points, points, points, samples, pt, targets)


def invert_block(block, store, note):
    groups = [block[8 * v : 8 * v + 8, :] for v in range(16)]
    lane = lax.broadcasted_iota(jnp.int32, (8, 128), 1)
    pivots = jnp.ones((8, 128), F32)
    spread = lambda a: jnp.broadcast_to(a, (8, 128))
    for g in range(32):
        j = 4 * g
        v, s = j // 8, j % 8
        inside = (lane >= j) & (lane < j + 4)
        raw = [spread(groups[v][s + a : s + a + 1, :]) for a in range(4)]
        p = [[spread(raw[a][:, j + b : j + b + 1]) for b in range(a + 1)] for a in range(4)]
        live = [u for u in range(v, 16) if not (u == v and s == 4)]
        cols = {u: [spread(groups[u][:, j + b : j + b + 1]) for b in range(4)] for u in live}
        d0 = p[0][0]
        i0 = 1.0 / d0
        l10, l20, l30 = p[1][0] * i0, p[2][0] * i0, p[3][0] * i0
        d1 = p[1][1] - l10 * p[1][0]
        i1 = 1.0 / d1
        q21, q31 = p[2][1] - l20 * p[1][0], p[3][1] - l30 * p[1][0]
        l21, l31 = q21 * i1, q31 * i1
        d2 = p[2][2] - l20 * p[2][0] - l21 * q21
        i2 = 1.0 / d2
        q32 = p[3][2] - l30 * p[2][0] - l31 * q21
        l32 = q32 * i2
        d3 = p[3][3] - l30 * p[3][0] - l31 * q31 - l32 * q32
        i3 = 1.0 / d3
        r = [
            jnp.where(inside, jnp.where(lane == j + a, 1.0, 0.0), raw[a]) for a in range(4)
        ]
        r[1] = r[1] - l10 * r[0]
        r[2] = r[2] - l20 * r[0] - l21 * r[1]
        r[3] = r[3] - l30 * r[0] - l31 * r[1] - l32 * r[2]
        for a, d in enumerate((d0, d1, d2, d3)):
            store(j + a, r[a] * lax.rsqrt(d))
            pivots = jnp.where(lane == j + a, d, pivots)
        q3 = r[3] * i3
        q2 = r[2] * i2 - l32 * q3
        q1 = r[1] * i1 - l21 * q2 - l31 * q3
        q0 = r[0] * i0 - l10 * q1 - l20 * q2 - l30 * q3
        for u in live:
            c = cols[u]
            base = jnp.where(inside, 0.0, groups[u])
            groups[u] = base - (c[0] * q0 + c[1] * q1) - (c[2] * q2 + c[3] * q3)
    return pivots


def eliminate(k, work, piece, inverse_ref, at):
    lo, hi = 128 * k, 128 * k + 128
    base = lo - at

    def store(r, line):
        piece[r : r + 1, :] = line[:1, :]

    pivots = invert_block(work[base : base + 128, lo:hi], store, None)
    row = lax.broadcasted_iota(jnp.int32, (128, 128), 0)
    t = jnp.where(row >= lax.broadcasted_iota(jnp.int32, (128, 128), 1), piece[...], 0.0)
    rest = jnp.dot(t, work[base : base + 128, :], preferred_element_type=F32, precision=HI)
    parts = [rest[:, :lo]] * (lo > 0) + [t] + [rest[:, hi:]] * (hi < PB)
    u = jnp.concatenate(parts, axis=1)
    inverse_ref[base : base + 128, :] = jnp.where(
        lax.broadcasted_iota(jnp.int32, (128, PB), 1) < hi, u, 0.0
    )
    if hi == PB:
        return pivots, None
    away = lax.dot_general(u[:, hi:], u, TN, preferred_element_type=F32, precision=HI)
    column = lax.broadcasted_iota(jnp.int32, (PB - hi, PB), 1)
    kept = jnp.where((column >= lo) & (column < hi), 0.0, work[base + 128 :, :])
    return pivots, kept - away


def note_log(log_ref, pivots):
    log_ref[...] = jnp.sum(jnp.log(pivots)[:1, :], axis=1, keepdims=True)


def factor_first_kernel(scale_ref, panel_ref, top_ref, inverse_ref, log_ref, left_ref, work, piece):
    i2, offset, over, jit = scale_ref[0], scale_ref[1], scale_ref[2], scale_ref[3]
    half = half_norm(panel_ref[...])
    left = widen(panel_ref[...], half + offset, True)
    right = widen(panel_ref[...], half, False)
    kern = jnp.exp2(i2 * lax.dot_general(left, right, NT, preferred_element_type=F32))
    row = lax.broadcasted_iota(jnp.int32, (PB, PB), 0)
    col = lax.broadcasted_iota(jnp.int32, (PB, PB), 1)
    top = jnp.concatenate([top_ref[l, :64, :] for l in range(PB // 64)], axis=0)
    work[...] = kern + jnp.where(row == col, jit, 0.0) + top * over
    pivots, left_over = eliminate(0, work, piece, inverse_ref, 0)
    note_log(log_ref, pivots)
    left_ref[...] = left_over


def factor_next_kernel(k, blocks, work_ref, inverse_ref, log_ref, *rest):
    work, piece = rest[-2], rest[-1]
    total = jnp.zeros((8, 128), F32)
    current = work_ref
    for step in range(blocks):
        pivots, left_over = eliminate(k + step, current, piece, inverse_ref, 128 * k)
        total = total + jnp.log(pivots)
        if step + 1 < blocks:
            work[128 * (step + 1) :, :] = left_over
            current = work
    log_ref[...] = jnp.sum(total[:1, :], axis=1, keepdims=True)
    if left_over is not None:
        rest[0][...] = left_over


def factor_first(scales, panel, top):
    full = pl.BlockSpec(memory_space=pltpu.VMEM)
    return pl.pallas_call(
        factor_first_kernel,
        out_shape=(
            jax.ShapeDtypeStruct((128, PB), F32),
            jax.ShapeDtypeStruct((1, 1), F32),
            jax.ShapeDtypeStruct((PB - 128, PB), F32),
        ),
        in_specs=[pl.BlockSpec(memory_space=pltpu.SMEM), full, full],
        out_specs=(full, full, full),
        scratch_shapes=[pltpu.VMEM((PB, PB), F32), pltpu.VMEM((128, 128), F32)],
        compiler_params=vmem(),
        cost_estimate=pl.CostEstimate(flops=6 * 10**9, bytes_accessed=2 << 20, transcendentals=1 << 18),
        name="factor_first",
    )(scales, panel, top)


def factor_next(k, blocks, work):
    full = pl.BlockSpec(memory_space=pltpu.VMEM)
    left = PB - 128 * (k + blocks)
    shapes = [jax.ShapeDtypeStruct((128 * blocks, PB), F32), jax.ShapeDtypeStruct((1, 1), F32)]
    if left:
        shapes.append(jax.ShapeDtypeStruct((left, PB), F32))
    return pl.pallas_call(
        functools.partial(factor_next_kernel, k, blocks),
        out_shape=tuple(shapes),
        in_specs=[full],
        out_specs=(full,) * len(shapes),
        scratch_shapes=[pltpu.VMEM(work.shape, F32), pltpu.VMEM((128, 128), F32)],
        compiler_params=vmem(),
        cost_estimate=pl.CostEstimate(flops=blocks * 5 * 10**9, bytes_accessed=2 << 20, transcendentals=1 << 18),
        name="factor_next",
    )(work)


def finish_kernel(ids_ref, scale_ref, own_ref, panel_ref, kept_ref, got_ref, right_ref, *rest):
    inverse_refs, (pf_ref, rhs_ref, sol_ref) = rest[:-3], rest[-3:]
    i2, offset, over, jit = scale_ref[0], scale_ref[1], scale_ref[2], scale_ref[3]
    rows = own_ref.shape[0]
    left = widen(own_ref[...], half_norm(own_ref[...]) + offset, True)
    right = widen(panel_ref[...], half_norm(panel_ref[...]), False)
    kern = jnp.exp2(i2 * lax.dot_general(left, right, NT, preferred_element_type=F32))
    row = ids_ref[2] + lax.broadcasted_iota(jnp.int32, (rows, PB), 0)
    col = lax.broadcasted_iota(jnp.int32, (rows, PB), 1)
    sums = kept_ref[...] + got_ref[...]
    system = kern + jnp.where(row == col, jit, 0.0) + sums[:rows, :] * over
    both = jnp.concatenate([system, right_ref[...] * over], axis=0)
    inverse = jnp.concatenate([r[...] for r in inverse_refs], axis=0)
    solved = lax.dot_general(both, inverse, NT, preferred_element_type=F32, precision=HI)
    pf = solved[:rows, :]
    sol = solved[rows:, :]
    pf_ref[...] = pf
    sol_ref[...] = sol[:1, :]
    back = lax.dot_general(sol, pf, NT, preferred_element_type=F32, precision=HI)
    rhs_ref[...] = sums[rows : rows + 1, :rows] * over - back[:1, :]


def finish(ids, scales, inducing, panel, kept, got, right, *inverse):
    rows = inducing.shape[0] // SHARDS
    smem = pl.BlockSpec(memory_space=pltpu.SMEM)
    full = lambda a: pl.BlockSpec(a.shape, lambda i, d: (0,) * a.ndim)
    return pl.pallas_call(
        finish_kernel,
        out_shape=(
            jax.ShapeDtypeStruct((rows, PB), F32),
            jax.ShapeDtypeStruct((1, rows), F32),
            jax.ShapeDtypeStruct((1, PB), F32),
        ),
        grid_spec=pltpu.PrefetchScalarGridSpec(
            num_scalar_prefetch=1,
            grid=(1,),
            in_specs=[smem, pl.BlockSpec((rows, 128), lambda i, d: (d[0], 0))]
            + [full(a) for a in (panel, kept, got, right) + inverse],
            out_specs=(
                pl.BlockSpec((rows, PB), lambda i, d: (0, 0)),
                pl.BlockSpec((1, rows), lambda i, d: (0, 0)),
                pl.BlockSpec((1, PB), lambda i, d: (0, 0)),
            ),
        ),
        compiler_params=vmem(),
        cost_estimate=pl.CostEstimate(flops=10**9, bytes_accessed=2 << 20, transcendentals=1 << 16),
        name="finish",
    )(ids, scales, inducing, panel, kept, got, right, *inverse)


def moved(x, axis, pairs):
    return lax.ppermute(x, axis, pairs)


def across(x, to):
    return lax.ppermute(x, "dp", [(i, to(i)) for i in range(SHARDS)])


def other_core(i):
    return i ^ 1


def along_x(i, k):
    return (i // 8) * 8 + (i + 2 * k) % 8


def along_y(i, k):
    return (i + 8 * k) % SHARDS


def gray(v):
    return v ^ (v >> 1)


def flipped(i, bit):
    y, x, c = i // 8, (i // 2) % 4, i % 2
    gx, gy = gray(x), gray(y)
    if bit == 0:
        c = c ^ 1
    elif bit < 3:
        gx = gx ^ bit
    else:
        gy = gy ^ (bit - 2)
    return gray(gy) * 8 + gray(gx) * 2 + c


def block_order(shard):
    r = jnp.arange(SHARDS, dtype=jnp.int32)
    y, x, c = shard // 8, (shard // 2) % 4, shard % 2
    gx = gray(x) ^ (((r >> 3) & 1) | (((r >> 2) & 1) << 1))
    gy = gray(y) ^ (((r >> 1) & 1) | ((r & 1) << 1))
    return (gray(gy) * 8 + gray(gx) * 2 + (c ^ (r >> 4))).astype(jnp.int32)


def after(x, *first):
    return lax.optimization_barrier((x,) + first)[0]


def sum_over(x, step):
    a, b, c = (across(x, functools.partial(step, k=k)) for k in (1, 2, 3))
    return (x + a) + (b + c)


def every_layer(half, layer):
    parts = jnp.zeros((LAYERS,) + half.shape, F32)
    ahead = behind = half
    parts = lax.dynamic_update_index_in_dim(parts, half, layer, 0)
    up = [(i, (i + 1) % LAYERS) for i in range(LAYERS)]
    down = [(i, (i - 1) % LAYERS) for i in range(LAYERS)]
    for k in range(1, 5):
        ahead = moved(ahead, "ind", up)
        parts = lax.dynamic_update_index_in_dim(parts, ahead, (layer - k) % LAYERS, 0)
        if k < 4:
            behind = moved(behind, "ind", down)
            parts = lax.dynamic_update_index_in_dim(parts, behind, (layer + k) % LAYERS, 0)
    return parts


def body(
    inputs, targets, row_counts, w_in, w_mid, w_out, feat_gain, inducing, log_scale, lengthscale, noise_var
):
    shard = lax.axis_index("dp").astype(jnp.int32)
    layer = lax.axis_index("ind").astype(jnp.int32)
    core = shard % 2
    slots = inputs.shape[0]
    own_rows = inducing.shape[0] // SHARDS
    ids = jnp.stack([shard, layer, layer * inducing.shape[0] + shard * own_rows]).astype(jnp.int32)
    order = block_order(shard)
    inv_sq = 1.0 / (lengthscale[0] * lengthscale[0])
    scales = jnp.stack(
        [inv_sq * LOG2E, log_scale[0] / inv_sq, 1.0 / noise_var[0], jnp.asarray(JITTER, F32)]
    )
    trow = targets.astype(F32).reshape(1, slots)
    network = (w_in, w_mid, w_out, feat_gain.reshape(1, -1))

    panel = inducing[:PB]
    far = [moved(panel, "ind", [(0, 3)]), moved(panel, "ind", [(0, 5)])]
    samples = embed(0, 2, ids, row_counts, inputs, *network)
    panel = jnp.where(layer == 3, far[0], jnp.where(layer == 5, far[1], panel))
    panel = after(panel, samples)
    near = [
        moved(panel, "ind", [(0, 1), (3, 4), (5, 6)]),
        moved(panel, "ind", [(0, 7), (3, 2)]),
    ]
    samples = embed(2, 2, ids, row_counts, after(inputs, panel), *network, before=samples)
    in_first = (layer == 1) | (layer == 4) | (layer == 6)
    in_second = (layer == 7) | (layer == 2)
    panel = jnp.where(in_first, near[0], jnp.where(in_second, near[1], panel))

    pt, top = panel_top(ids, scales, samples, panel, trow)
    half = lax.dynamic_index_in_dim(top, core, 0, False)
    sent = lax.dynamic_index_in_dim(top, 1 - core, 0, False)
    away = gram(after(order[16:], sent), scales, inducing, samples, pt, trow)
    half = half + across(sent, other_core)
    got = across(away, other_core)
    half = after(half, away)
    half = sum_over(half, along_x)
    kept = gram(order[:16], scales, inducing, samples, pt, trow)
    send = kept[8:] + got[8:]
    half = after(half, send)
    half = sum_over(half, along_y)
    kept, got = kept[:8] + got[:8], across(send, functools.partial(flipped, bit=1))
    parts = every_layer(half, layer)
    other = across(parts, other_core)
    left = jnp.where(core == 0, parts, other)
    right = jnp.where(core == 0, other, parts)
    whole = jnp.concatenate([left, right], axis=2)

    send = kept[4:] + got[4:]
    kept, got = kept[:4] + got[:4], across(send, functools.partial(flipped, bit=2))
    inverse0, log0, work = factor_first(scales, panel, whole)
    got = after(got, work)
    send = kept[2:] + got[2:]
    kept, got = kept[:2] + got[:2], across(send, functools.partial(flipped, bit=3))
    inverse1, log1, work = factor_next(1, 1, work)
    got = after(got, work)
    send = kept[1:] + got[1:]
    kept, got = kept[:1] + got[:1], across(send, functools.partial(flipped, bit=4))
    inverse2, log2 = factor_next(2, 2, work)
    pf, rhs, sol = finish(
        ids, scales, inducing, panel, kept[0], got[0], whole[0, 64:], inverse0, inverse1, inverse2
    )
    return pf, rhs.reshape(own_rows), sol.reshape(PB), (log0 + log1 + log2).reshape(1)


def solution(mesh):
    return jax.shard_map(
        body,
        mesh=mesh,
        in_specs=(P("dp", None), P("dp"), P(), P(), P(), P(), P(), P("ind", None), P(), P(), P()),
        out_specs=(P(("ind", "dp"), None), P(("ind", "dp")), P(), P()),
        check_vma=False,
    )
```

```python
import functools
import jax
import jax.numpy as jnp
from jax import lax
from jax.experimental import pallas as pl
from jax.experimental.pallas import tpu as pltpu
from jax.sharding import PartitionSpec as P


PB = 512
JITTER = 0.0001
SHARDS, LAYERS = 32, 8
LOG2E = 1.4426950408889634
MASKED = -1.0e6
F32, BF16 = jnp.float32, jnp.bfloat16
HI = lax.Precision.HIGHEST
NT = (((1,), (1,)), ((), ()))
TN = (((0,), (0,)), ((), ()))


def vmem(limit=60 << 20):
    return pltpu.CompilerParams(vmem_limit_bytes=limit)


def widen(points, half, first):
    rows = points.shape[0]
    high = half.astype(BF16)
    rest = half - high.astype(F32)
    mid = rest.astype(BF16)
    low = (rest - mid.astype(F32)).astype(BF16)
    lane = lax.broadcasted_iota(jnp.int32, (rows, 128), 1)
    at = 0 if first else 3
    one = 3 if first else 0
    tail = jnp.where((lane >= one) & (lane < one + 3), 1.0, 0.0)
    tail = jnp.where(lane == at, high.astype(F32), tail)
    tail = jnp.where(lane == at + 1, mid.astype(F32), tail)
    tail = jnp.where(lane == at + 2, low.astype(F32), tail)
    return jnp.concatenate([points, tail.astype(BF16)], axis=1)


def half_norm(points):
    wide = points.astype(F32)
    return -0.5 * jnp.sum(wide * wide, axis=1, keepdims=True)


def gelu(x):
    inner = x * (0.7978845608028654 + 0.035677408136300125 * (x * x))
    half = 0.5 * x
    return half + half * jnp.tanh(inner)


def embed_kernel(base, ids_ref, counts_ref, x_ref, w1_ref, w2_ref, w3_ref, gain_ref, *rest):
    out_ref = rest[-1]
    rows = x_ref.shape[0]
    one = gelu(jnp.dot(x_ref[...], w1_ref[...], preferred_element_type=F32)).astype(BF16)
    two = gelu(jnp.dot(one, w2_ref[...], preferred_element_type=F32)).astype(BF16)
    proj = jnp.dot(two, w3_ref[...], preferred_element_type=F32)
    mean = jnp.mean(proj * proj, axis=1, keepdims=True)
    points = (proj * lax.rsqrt(mean + 1e-06) * gain_ref[...]).astype(BF16)
    index = (base + pl.program_id(0)) * rows + lax.broadcasted_iota(jnp.int32, (rows, 1), 0)
    half = jnp.where(index < counts_ref[ids_ref[0]], half_norm(points), MASKED)
    out_ref[...] = widen(points, half, False)


def embed(base, steps, ids, counts, inputs, w_in, w_mid, w_out, gain, before=None, tile=512):
    slots = inputs.shape[0]
    whole = lambda a: pl.BlockSpec(a.shape, lambda i: (0, 0), pipeline_mode=pl.Buffered(1))
    smem = pl.BlockSpec(memory_space=pltpu.SMEM)
    more = () if before is None else (before,)
    return pl.pallas_call(
        functools.partial(embed_kernel, base),
        out_shape=jax.ShapeDtypeStruct((slots, 256), BF16),
        grid=(steps,),
        in_specs=[
            smem,
            smem,
            pl.BlockSpec((tile, inputs.shape[1]), lambda i: (i + base, 0)),
            whole(w_in),
            whole(w_mid),
            whole(w_out),
            whole(gain),
        ]
        + [pl.BlockSpec(memory_space=pl.ANY)] * len(more),
        out_specs=pl.BlockSpec((tile, 256), lambda i: (i + base, 0)),
        input_output_aliases={7: 0} if more else {},
        compiler_params=vmem(),
        cost_estimate=pl.CostEstimate(
            flops=steps * 15 * 10**8, bytes_accessed=4 << 20, transcendentals=steps << 20
        ),
        name="embed",
    )(ids, counts, inputs, w_in, w_mid, w_out, gain, *more)


WIDE = PB + 128


def panel_kernel(ids_ref, scale_ref, samples_ref, panel_ref, t_ref, pt_ref, top_ref, total, crossed):
    step = pl.program_id(0)
    i2, offset = scale_ref[0], scale_ref[1]
    share = ids_ref[1] % 4
    samples = samples_ref[...]
    panel = widen(panel_ref[...], half_norm(panel_ref[...]) + offset, True)
    mine = jnp.concatenate(
        [
            panel_ref[pl.ds(pl.multiple_of(share * 64, 64), 64), :],
            panel_ref[pl.ds(pl.multiple_of((7 - share) * 64, 64), 64), :],
        ],
        axis=0,
    )
    chunk = widen(mine, half_norm(mine) + offset, True)
    kern = jnp.exp2(i2 * lax.dot_general(samples, panel, NT, preferred_element_type=F32)).astype(BF16)
    part = jnp.exp2(i2 * lax.dot_general(chunk, samples, NT, preferred_element_type=F32)).astype(BF16)
    pt_ref[...] = kern
    sums = jnp.dot(part, kern, preferred_element_type=F32)
    cross = jnp.sum(part.astype(F32) * t_ref[...], axis=1, keepdims=True)
    cross = jnp.broadcast_to(cross, (128, 128))

    @pl.when(step == 0)
    def _():
        total[...] = sums
        crossed[...] = cross

    @pl.when(step > 0)
    def _():
        total[...] += sums
        crossed[...] += cross

    for s in range(4):

        @pl.when((step == pl.num_programs(0) - 1) & (share == s))
        def _(s=s):
            packed = jnp.concatenate(
                [
                    total[64:, : 64 * (8 - s)],
                    total[:64, : 64 * (s + 1)],
                    crossed[:64, :1],
                    crossed[64:, :1],
                    jnp.zeros((64, 62), F32),
                ],
                axis=1,
            )
            top_ref[0, :, :] = packed[:32, :]
            top_ref[1, :, :] = packed[32:, :]


def panel_top(ids, scales, samples, panel, targets, tile=512):
    slots = samples.shape[0]
    smem = pl.BlockSpec(memory_space=pltpu.SMEM)
    return pl.pallas_call(
        panel_kernel,
        out_shape=(jax.ShapeDtypeStruct((slots, PB), BF16), jax.ShapeDtypeStruct((2, 32, WIDE), F32)),
        grid=(slots // tile,),
        in_specs=[
            smem,
            smem,
            pl.BlockSpec((tile, 256), lambda i: (i, 0)),
            pl.BlockSpec(panel.shape, lambda i: (0, 0)),
            pl.BlockSpec((1, tile), lambda i: (0, i)),
        ],
        out_specs=(
            pl.BlockSpec((tile, PB), lambda i: (i, 0)),
            pl.BlockSpec((2, 32, WIDE), lambda i: (0, 0, 0)),
        ),
        scratch_shapes=[pltpu.VMEM((128, PB), F32), pltpu.VMEM((128, 128), F32)],
        compiler_params=vmem(),
        cost_estimate=pl.CostEstimate(flops=15 * 10**8, bytes_accessed=4 << 20, transcendentals=1 << 20),
        name="panel",
    )(ids, scales, samples, panel, targets)


def gram_kernel(order_ref, scale_ref, *refs):
    points_refs, (samples_ref, pt_ref, t_ref, out_ref) = refs[:4], refs[4:]
    i2, offset = scale_ref[0], scale_ref[1]
    raw = jnp.concatenate([p[...] for p in points_refs], axis=0)
    points = widen(raw, half_norm(raw) + offset, True)
    kern = jnp.exp2(
        i2 * lax.dot_general(points, samples_ref[...], NT, preferred_element_type=F32)
    ).astype(BF16)
    crossed = jnp.sum(kern.astype(F32) * t_ref[...], axis=1, keepdims=True)
    crossed = jnp.broadcast_to(crossed, (256, 128)).T
    sums = jnp.dot(kern, pt_ref[...], preferred_element_type=F32)
    for b in range(4):
        out_ref[b, :64, :] = sums[b * 64 : b * 64 + 64, :]
        out_ref[b, 64:, :] = jnp.concatenate(
            [crossed[:8, b * 64 : b * 64 + 64], jnp.zeros((8, PB - 64), F32)], axis=1
        )


def gram(order, scales, points, samples, pt, targets):
    count = order.shape[0]
    whole = lambda a: pl.BlockSpec(a.shape, lambda i, o: (0, 0), pipeline_mode=pl.Buffered(1))
    block = lambda q: pl.BlockSpec((64, 128), lambda i, o: (o[4 * i + q], 0))
    return pl.pallas_call(
        gram_kernel,
        out_shape=jax.ShapeDtypeStruct((count, 72, PB), F32),
        grid_spec=pltpu.PrefetchScalarGridSpec(
            num_scalar_prefetch=1,
            grid=(count // 4,),
            in_specs=[pl.BlockSpec(memory_space=pltpu.SMEM)]
            + [block(q) for q in range(4)]
            + [whole(samples), whole(pt), whole(targets)],
            out_specs=pl.BlockSpec((4, 72, PB), lambda i, o: (i, 0, 0)),
        ),
        compiler_params=vmem(),
        cost_estimate=pl.CostEstimate(flops=count * 2 * 10**8, bytes_accessed=6 << 20, transcendentals=2 << 20),
        name="gram",
    )(order, scales, points, points, points, points, samples, pt, targets)


def invert_block(block, store):
    groups = [block[8 * v : 8 * v + 8, :] for v in range(16)]
    lane = lax.broadcasted_iota(jnp.int32, (8, 128), 1)
    pivots = jnp.ones((8, 128), F32)
    spread = lambda a: jnp.broadcast_to(a, (8, 128))
    for g in range(16):
        j = 8 * g
        inside = (lane >= j) & (lane < j + 8)
        local = [spread(groups[g][:, j + b : j + b + 1]) for b in range(8)]
        p = [[spread(local[b][a : a + 1, :]) for b in range(a + 1)] for a in range(8)]
        cols = [[spread(groups[u][:, j + b : j + b + 1]) for b in range(8)] for u in range(g + 1, 16)]
        r = [
            jnp.where(inside, jnp.where(lane == j + a, 1.0, 0.0), spread(groups[g][a : a + 1, :]))
            for a in range(8)
        ]
        inv = []
        low = [[None] * 8 for _ in range(8)]
        for m in range(8):
            d = p[m][m]
            inv.append(1.0 / d)
            store(j + m, r[m] * lax.rsqrt(d))
            pivots = jnp.where(lane == j + m, d, pivots)
            for a in range(m + 1, 8):
                low[a][m] = p[a][m] * inv[m]
                r[a] = r[a] - low[a][m] * r[m]
                for b in range(m + 1, a):
                    p[a][b] = p[a][b] - low[a][m] * p[b][m]
                p[a][a] = p[a][a] - (p[a][m] * p[a][m]) * inv[m]
        q = [r[a] * inv[a] for a in range(8)]
        for b in range(7, 0, -1):
            for a in range(b):
                q[a] = q[a] - low[b][a] * q[b]
        for u in range(g + 1, 16):
            c = cols[u - g - 1]
            base = jnp.where(inside, 0.0, groups[u])
            for b in range(7, -1, -1):
                base = base - c[b] * q[b]
            groups[u] = base
    return pivots


def inverse_of(block, piece):
    def store(r, line):
        piece[r : r + 1, :] = line[:1, :]

    pivots = invert_block(block, store)
    row = lax.broadcasted_iota(jnp.int32, (128, 128), 0)
    lower = row >= lax.broadcasted_iota(jnp.int32, (128, 128), 1)
    return jnp.where(lower, piece[...], 0.0), jnp.log(pivots)


def factor_first_kernel(
    ids_ref, scale_ref, panel_ref, mine_ref, other_ref, inverse_ref, log_ref, left_ref, right_ref, work, piece
):
    i2, offset, over, jit = scale_ref[0], scale_ref[1], scale_ref[2], scale_ref[3]
    first = ids_ref[0] % 2 == 0
    for s in range(4):
        place = (s + 8 - ids_ref[1]) % 4
        mine, other = mine_ref[place], other_ref[place]
        share = jnp.concatenate([jnp.where(first, mine, other), jnp.where(first, other, mine)], axis=0)
        wide, slim = 64 * (8 - s), 64 * (s + 1)
        work[wide - 64 : wide, :wide] = share[:, :wide]
        work[slim - 64 : slim, :slim] = share[:, wide : wide + slim]
        if wide < PB:
            work[wide - 64 : wide, wide:] = jnp.zeros((64, PB - wide), F32)
        work[slim - 64 : slim, slim:] = jnp.zeros((64, PB - slim), F32)
        cross = share[:, PB:].T
        right_ref[:, slim - 64 : slim] = cross[64:65, :] * over
        right_ref[:, wide - 64 : wide] = cross[65:66, :] * over
    half = half_norm(panel_ref[...])
    left = widen(panel_ref[...], half + offset, True)
    right = widen(panel_ref[...], half, False)
    kern = jnp.exp2(i2 * lax.dot_general(left, right, NT, preferred_element_type=F32))
    row = lax.broadcasted_iota(jnp.int32, (PB, PB), 0)
    col = lax.broadcasted_iota(jnp.int32, (PB, PB), 1)
    lower = work[...]
    top = jnp.where(row >= col, lower, lower.T)
    work[...] = kern + jnp.where(row == col, jit, 0.0) + top * over
    t, logs = inverse_of(work[:128, :128], piece)
    rest = jnp.dot(t, work[:128, 128:], preferred_element_type=F32, precision=HI)
    u = jnp.concatenate([t, rest], axis=1)
    inverse_ref[...] = jnp.where(lax.broadcasted_iota(jnp.int32, (128, PB), 1) < 128, u, 0.0)
    away = lax.dot_general(rest, u, TN, preferred_element_type=F32, precision=HI)
    column = lax.broadcasted_iota(jnp.int32, (PB - 128, PB), 1)
    left_ref[...] = jnp.where(column < 128, 0.0, work[128:, :]) - away
    log_ref[...] = jnp.sum(logs[:1, :], axis=1, keepdims=True)


def factor_next_kernel(work_ref, inverse_ref, log_ref, work, across_ref, piece):
    work[...] = work_ref[...]
    row = lax.broadcasted_iota(jnp.int32, (PB - 128, PB), 0)
    column = lax.broadcasted_iota(jnp.int32, (PB - 128, PB), 1)

    def one(k, total):
        lo = pl.multiple_of(128 * k, 128)
        rows = pl.ds(pl.multiple_of(128 * k - 128, 128), 128)
        t, logs = inverse_of(work[rows, pl.ds(lo, 128)], piece)
        across_ref[...] = jnp.dot(t, work[rows, :], preferred_element_type=F32, precision=HI)
        across_ref[:, pl.ds(lo, 128)] = t
        u = across_ref[...]
        inverse_ref[rows, :] = jnp.where(column[:128] < lo + 128, u, 0.0)
        away = lax.dot_general(u[:, 128:], u, TN, preferred_element_type=F32, precision=HI)
        inside = (column >= lo) & (column < lo + 128)
        left = jnp.where(inside, 0.0, work[...]) - away
        work[...] = jnp.where(row >= lo, left, work[...])
        return total + logs

    total = lax.fori_loop(1, PB // 128, one, jnp.zeros((8, 128), F32))
    log_ref[...] = jnp.sum(total[:1, :], axis=1, keepdims=True)


def factor_first(ids, scales, panel, mine, other):
    full = pl.BlockSpec(memory_space=pltpu.VMEM)
    smem = pl.BlockSpec(memory_space=pltpu.SMEM)
    return pl.pallas_call(
        factor_first_kernel,
        out_shape=(
            jax.ShapeDtypeStruct((128, PB), F32),
            jax.ShapeDtypeStruct((1, 1), F32),
            jax.ShapeDtypeStruct((PB - 128, PB), F32),
            jax.ShapeDtypeStruct((1, PB), F32),
        ),
        in_specs=[smem, smem, full, full, full],
        out_specs=(full,) * 4,
        scratch_shapes=[pltpu.VMEM((PB, PB), F32), pltpu.VMEM((128, 128), F32)],
        compiler_params=vmem(),
        cost_estimate=pl.CostEstimate(flops=6 * 10**9, bytes_accessed=2 << 20, transcendentals=1 << 18),
        name="factor_first",
    )(ids, scales, panel, mine, other)


def factor_next(work):
    full = pl.BlockSpec(memory_space=pltpu.VMEM)
    return pl.pallas_call(
        factor_next_kernel,
        out_shape=(jax.ShapeDtypeStruct(work.shape, F32), jax.ShapeDtypeStruct((1, 1), F32)),
        in_specs=[full],
        out_specs=(full, full),
        scratch_shapes=[pltpu.VMEM(work.shape, F32), pltpu.VMEM((128, PB), F32), pltpu.VMEM((128, 128), F32)],
        compiler_params=vmem(),
        cost_estimate=pl.CostEstimate(flops=15 * 10**9, bytes_accessed=2 << 20, transcendentals=1 << 18),
        name="factor_next",
    )(work)


def finish_kernel(ids_ref, scale_ref, own_ref, panel_ref, right_ref, inverse0_ref, inverse1_ref, *rest):
    parts, (pf_ref, rhs_ref, sol_ref) = rest[:-3], rest[-3:]
    i2, offset, over, jit = scale_ref[0], scale_ref[1], scale_ref[2], scale_ref[3]
    rows = own_ref.shape[0]
    left = widen(own_ref[...], half_norm(own_ref[...]) + offset, True)
    right = widen(panel_ref[...], half_norm(panel_ref[...]), False)
    kern = jnp.exp2(i2 * lax.dot_general(left, right, NT, preferred_element_type=F32))
    row = ids_ref[2] + lax.broadcasted_iota(jnp.int32, (rows, PB), 0)
    col = lax.broadcasted_iota(jnp.int32, (rows, PB), 1)
    a, b, c, d = (p[...] for p in parts)
    sums = (a + b) + (c + d)
    system = kern + jnp.where(row == col, jit, 0.0) + sums[:rows, :] * over
    both = jnp.concatenate([system, jnp.broadcast_to(right_ref[...], (8, PB))], axis=0)
    inverse = jnp.concatenate([inverse0_ref[...], inverse1_ref[...]], axis=0)
    solved = lax.dot_general(both, inverse, NT, preferred_element_type=F32, precision=HI)
    pf = solved[:rows, :]
    sol = solved[rows:, :]
    pf_ref[...] = pf
    sol_ref[...] = sol[:1, :]
    back = lax.dot_general(sol, pf, NT, preferred_element_type=F32, precision=HI)
    rhs_ref[...] = sums[rows : rows + 1, :rows] * over - back[:1, :]


def finish(ids, scales, inducing, panel, *others):
    rows = inducing.shape[0] // SHARDS
    smem = pl.BlockSpec(memory_space=pltpu.SMEM)
    full = lambda a: pl.BlockSpec(a.shape, lambda i, d: (0,) * a.ndim)
    return pl.pallas_call(
        finish_kernel,
        out_shape=(
            jax.ShapeDtypeStruct((rows, PB), F32),
            jax.ShapeDtypeStruct((1, rows), F32),
            jax.ShapeDtypeStruct((1, PB), F32),
        ),
        grid_spec=pltpu.PrefetchScalarGridSpec(
            num_scalar_prefetch=1,
            grid=(1,),
            in_specs=[smem, pl.BlockSpec((rows, 128), lambda i, d: (d[0], 0))]
            + [full(a) for a in (panel,) + others],
            out_specs=(
                pl.BlockSpec((rows, PB), lambda i, d: (0, 0)),
                pl.BlockSpec((1, rows), lambda i, d: (0, 0)),
                pl.BlockSpec((1, PB), lambda i, d: (0, 0)),
            ),
        ),
        compiler_params=vmem(),
        cost_estimate=pl.CostEstimate(flops=10**9, bytes_accessed=2 << 20, transcendentals=1 << 16),
        name="finish",
    )(ids, scales, inducing, panel, *others)


def moved(x, axis, pairs):
    return lax.ppermute(x, axis, pairs)


def across(x, to):
    return lax.ppermute(x, "dp", [(i, to(i)) for i in range(SHARDS)])


def other_core(i):
    return i ^ 1


def along_x(i, k):
    return (i // 8) * 8 + (i + 2 * k) % 8


def along_y(i, k):
    return (i + 8 * k) % SHARDS


def gray(v):
    return v ^ (v >> 1)


def place_of(i):
    return i % 2, gray((i // 2) % 4), gray(i // 8)


def device_at(c, gx, gy):
    return gray(gy) * 8 + gray(gx) * 2 + c


def flipped(i, bit, which):
    c, gx, gy = place_of(i)
    return device_at(c, gx ^ (bit * (which >> 1)), gy ^ (bit * (which & 1)))


def block_order(shard):
    r = jnp.arange(SHARDS, dtype=jnp.int32)
    c, gx, gy = place_of(shard)
    gx = gx ^ (((r >> 3) & 1) | (((r >> 1) & 1) << 1))
    gy = gy ^ (((r >> 2) & 1) | ((r & 1) << 1))
    return device_at(c ^ (r >> 4), gx, gy).astype(jnp.int32)


def quarters(*parts):
    n = parts[0].shape[0] // 4
    return [sum(p[n * w : n * w + n] for p in parts) for w in range(4)]


def spread_blocks(sent, bit):
    return [sent[0]] + [
        across(sent[w], functools.partial(flipped, bit=bit, which=w)) for w in (3, 2, 1)
    ]


def after(x, *first):
    return lax.optimization_barrier((x,) + first)[0]


def sum_over(x, step):
    a, b, c = (across(x, functools.partial(step, k=k)) for k in (1, 2, 3))
    return (x + a) + (b + c)


def every_share(half):
    ring = lambda k: moved(half, "ind", [(i, (i - k) % LAYERS) for i in range(LAYERS)])
    return jnp.stack([half, ring(1), ring(2), ring(-1)])


def body(
    inputs, targets, row_counts, w_in, w_mid, w_out, feat_gain, inducing, log_scale, lengthscale, noise_var
):
    shard = lax.axis_index("dp").astype(jnp.int32)
    layer = lax.axis_index("ind").astype(jnp.int32)
    core = shard % 2
    slots = inputs.shape[0]
    own_rows = inducing.shape[0] // SHARDS
    ids = jnp.stack([shard, layer, layer * inducing.shape[0] + shard * own_rows]).astype(jnp.int32)
    order = block_order(shard)
    inv_sq = 1.0 / (lengthscale[0] * lengthscale[0])
    scales = jnp.stack(
        [inv_sq * LOG2E, log_scale[0] / inv_sq, 1.0 / noise_var[0], jnp.asarray(JITTER, F32)]
    )
    trow = targets.astype(F32).reshape(1, slots)
    network = (w_in, w_mid, w_out, feat_gain.reshape(1, -1))

    panel = inducing[:PB]
    far = [moved(panel, "ind", [(0, 3)]), moved(panel, "ind", [(0, 5)])]
    samples = embed(0, 2, ids, row_counts, inputs, *network)
    panel = jnp.where(layer == 3, far[0], jnp.where(layer == 5, far[1], panel))
    panel = after(panel, samples)
    near = [
        moved(panel, "ind", [(0, 1), (3, 4), (5, 6)]),
        moved(panel, "ind", [(0, 7), (3, 2)]),
    ]
    samples = embed(2, 2, ids, row_counts, after(inputs, panel), *network, before=samples)
    in_first = (layer == 1) | (layer == 4) | (layer == 6)
    in_second = (layer == 7) | (layer == 2)
    panel = jnp.where(in_first, near[0], jnp.where(in_second, near[1], panel))

    pt, top = panel_top(ids, scales, samples, panel, trow)
    sent = lax.dynamic_index_in_dim(top, 1 - core, 0, False)
    away = gram(after(order[16:], sent), scales, inducing, samples, pt, trow)
    half = lax.dynamic_index_in_dim(top, core, 0, False) + across(sent, other_core)
    got = across(after(away, half), other_core)
    half = after(half, away)
    half = sum_over(half, along_x)
    kept = gram(order[:16], scales, inducing, samples, pt, trow)
    half = sum_over(half, along_y)
    sums = quarters(kept, got)
    parts = spread_blocks(sums, 1)
    mine = every_share(half)
    other = across(mine, other_core)
    inverse0, log0, work, right = factor_first(ids, scales, panel, mine, other)
    parts = spread_blocks(quarters(after(parts[0], work), *parts[1:]), 2)
    inverse1, log1 = factor_next(work)
    pf, rhs, sol = finish(
        ids, scales, inducing, panel, right, inverse0, inverse1, *(p[0] for p in parts)
    )
    return pf, rhs.reshape(own_rows), sol.reshape(PB), (log0 + log1).reshape(1)


def solution(mesh):
    return jax.shard_map(
        body,
        mesh=mesh,
        in_specs=(P("dp", None), P("dp"), P(), P(), P(), P(), P(), P("ind", None), P(), P(), P()),
        out_specs=(P(("ind", "dp"), None), P(("ind", "dp")), P(), P()),
        check_vma=False,
    )
```

```python
import functools
import jax
import jax.numpy as jnp
from jax import lax
from jax.experimental import pallas as pl
from jax.experimental.pallas import tpu as pltpu
from jax.sharding import PartitionSpec as P


PB = 512
JITTER = 0.0001
SHARDS, LAYERS = 32, 8
LOG2E = 1.4426950408889634
MASKED = -1.0e6
F32, BF16 = jnp.float32, jnp.bfloat16
HI = lax.Precision.HIGHEST
NT = (((1,), (1,)), ((), ()))
TN = (((0,), (0,)), ((), ()))


def vmem(limit=60 << 20):
    return pltpu.CompilerParams(vmem_limit_bytes=limit)


def scales(log_ref, length_ref):
    square = length_ref[...] * length_ref[...]
    return LOG2E / square, log_ref[...] * square


def single():
    return pl.BlockSpec((1, 1), lambda *at: (0, 0))


def widen(points, half, first):
    rows = points.shape[0]
    high = half.astype(BF16)
    rest = half - high.astype(F32)
    mid = rest.astype(BF16)
    low = (rest - mid.astype(F32)).astype(BF16)
    lane = lax.broadcasted_iota(jnp.int32, (rows, 128), 1)
    at = 0 if first else 3
    one = 3 if first else 0
    tail = jnp.where((lane >= one) & (lane < one + 3), 1.0, 0.0)
    tail = jnp.where(lane == at, high.astype(F32), tail)
    tail = jnp.where(lane == at + 1, mid.astype(F32), tail)
    tail = jnp.where(lane == at + 2, low.astype(F32), tail)
    return jnp.concatenate([points, tail.astype(BF16)], axis=1)


def half_norm(points):
    wide = points.astype(F32)
    return -0.5 * jnp.sum(wide * wide, axis=1, keepdims=True)


def gelu(x):
    inner = x * (0.7978845608028654 + 0.035677408136300125 * (x * x))
    half = 0.5 * x
    return half + half * jnp.tanh(inner)


def embed_kernel(base, ids_ref, counts_ref, x_ref, w1_ref, w2_ref, w3_ref, gain_ref, *rest):
    out_ref = rest[-1]
    rows = x_ref.shape[0]
    one = gelu(jnp.dot(x_ref[...], w1_ref[...], preferred_element_type=F32)).astype(BF16)
    two = gelu(jnp.dot(one, w2_ref[...], preferred_element_type=F32)).astype(BF16)
    proj = jnp.dot(two, w3_ref[...], preferred_element_type=F32)
    mean = jnp.mean(proj * proj, axis=1, keepdims=True)
    points = (proj * lax.rsqrt(mean + 1e-06) * gain_ref[...]).astype(BF16)
    index = (base + pl.program_id(0)) * rows + lax.broadcasted_iota(jnp.int32, (rows, 1), 0)
    half = jnp.where(index < counts_ref[ids_ref[32]], half_norm(points), MASKED)
    out_ref[...] = widen(points, half, False)


def embed(base, steps, ids, counts, inputs, w_in, w_mid, w_out, gain, before=None, tile=512):
    slots = inputs.shape[0]
    whole = lambda a: pl.BlockSpec(a.shape, lambda i: (0, 0), pipeline_mode=pl.Buffered(1))
    smem = pl.BlockSpec(memory_space=pltpu.SMEM)
    more = () if before is None else (before,)
    return pl.pallas_call(
        functools.partial(embed_kernel, base),
        out_shape=jax.ShapeDtypeStruct((slots, 256), BF16),
        grid=(steps,),
        in_specs=[
            smem,
            smem,
            pl.BlockSpec((tile, inputs.shape[1]), lambda i: (i + base, 0)),
            whole(w_in),
            whole(w_mid),
            whole(w_out),
            whole(gain),
        ]
        + [pl.BlockSpec(memory_space=pl.ANY)] * len(more),
        out_specs=pl.BlockSpec((tile, 256), lambda i: (i + base, 0)),
        input_output_aliases={7: 0} if more else {},
        compiler_params=vmem(),
        cost_estimate=pl.CostEstimate(
            flops=steps * 15 * 10**8, bytes_accessed=4 << 20, transcendentals=steps << 20
        ),
        name="embed",
    )(ids, counts, inputs, w_in, w_mid, w_out, gain, *more)


WIDE = PB + 128


def panel_kernel(
    ids_ref, log_ref, length_ref, samples_ref, panel_ref, t_ref, pt_ref, kept_ref, sent_ref, total, crossed
):
    step = pl.program_id(0)
    i2, offset = scales(log_ref, length_ref)
    share = ids_ref[33] % 4
    samples = samples_ref[...]
    panel = widen(panel_ref[...], half_norm(panel_ref[...]) + offset, True)
    mine = jnp.concatenate(
        [
            panel_ref[pl.ds(pl.multiple_of(share * 64, 64), 64), :],
            panel_ref[pl.ds(pl.multiple_of((7 - share) * 64, 64), 64), :],
        ],
        axis=0,
    )
    chunk = widen(mine, half_norm(mine) + offset, True)
    kern = jnp.exp2(i2 * lax.dot_general(samples, panel, NT, preferred_element_type=F32)).astype(BF16)
    part = jnp.exp2(i2 * lax.dot_general(chunk, samples, NT, preferred_element_type=F32)).astype(BF16)
    pt_ref[...] = kern
    sums = jnp.dot(part, kern, preferred_element_type=F32)
    cross = jnp.sum(part.astype(F32) * t_ref[...], axis=1, keepdims=True)
    cross = jnp.broadcast_to(cross, (128, 128))

    @pl.when(step == 0)
    def _():
        total[...] = sums
        crossed[...] = cross

    @pl.when(step > 0)
    def _():
        total[...] += sums
        crossed[...] += cross

    for s in range(4):

        @pl.when((step == pl.num_programs(0) - 1) & (share == s))
        def _(s=s):
            packed = jnp.concatenate(
                [
                    total[64:, : 64 * (8 - s)],
                    total[:64, : 64 * (s + 1)],
                    crossed[:64, :1],
                    crossed[64:, :1],
                    jnp.zeros((64, 62), F32),
                ],
                axis=1,
            )
            first = ids_ref[32] % 2 == 0
            kept_ref[...] = jnp.where(first, packed[:32, :], packed[32:, :])
            sent_ref[...] = jnp.where(first, packed[32:, :], packed[:32, :])


def panel_top(ids, log_scale, lengthscale, samples, panel, targets, tile=512):
    slots = samples.shape[0]
    smem = pl.BlockSpec(memory_space=pltpu.SMEM)
    return pl.pallas_call(
        panel_kernel,
        out_shape=(
            jax.ShapeDtypeStruct((slots, PB), BF16),
            jax.ShapeDtypeStruct((32, WIDE), F32),
            jax.ShapeDtypeStruct((32, WIDE), F32),
        ),
        grid=(slots // tile,),
        in_specs=[
            smem,
            single(),
            single(),
            pl.BlockSpec((tile, 256), lambda i: (i, 0)),
            pl.BlockSpec(panel.shape, lambda i: (0, 0)),
            pl.BlockSpec((1, tile), lambda i: (0, i)),
        ],
        out_specs=(
            pl.BlockSpec((tile, PB), lambda i: (i, 0)),
            pl.BlockSpec((32, WIDE), lambda i: (0, 0)),
            pl.BlockSpec((32, WIDE), lambda i: (0, 0)),
        ),
        scratch_shapes=[pltpu.VMEM((128, PB), F32), pltpu.VMEM((128, 128), F32)],
        compiler_params=vmem(),
        cost_estimate=pl.CostEstimate(flops=15 * 10**8, bytes_accessed=4 << 20, transcendentals=1 << 20),
        name="panel",
    )(ids, log_scale, lengthscale, samples, panel, targets)


def gram_kernel(ids_ref, log_ref, length_ref, *refs):
    points_refs, (samples_ref, pt_ref, t_ref, out_ref) = refs[:4], refs[4:]
    i2, offset = scales(log_ref, length_ref)
    raw = jnp.concatenate([p[...] for p in points_refs], axis=0)
    points = widen(raw, half_norm(raw) + offset, True)
    kern = jnp.exp2(
        i2 * lax.dot_general(points, samples_ref[...], NT, preferred_element_type=F32)
    ).astype(BF16)
    crossed = jnp.sum(kern.astype(F32) * t_ref[...], axis=1, keepdims=True)
    crossed = jnp.broadcast_to(crossed, (256, 128)).T
    sums = jnp.dot(kern, pt_ref[...], preferred_element_type=F32)
    for b in range(4):
        out_ref[b, :64, :] = sums[b * 64 : b * 64 + 64, :]
        out_ref[b, 64:, :] = jnp.concatenate(
            [crossed[:8, b * 64 : b * 64 + 64], jnp.zeros((8, PB - 64), F32)], axis=1
        )


def gram(ids, at, count, log_scale, lengthscale, points, samples, pt, targets):
    whole = lambda a: pl.BlockSpec(a.shape, lambda i, o: (0, 0), pipeline_mode=pl.Buffered(1))
    block = lambda q: pl.BlockSpec((64, 128), lambda i, o: (o[at + 4 * i + q], 0))
    return pl.pallas_call(
        gram_kernel,
        out_shape=jax.ShapeDtypeStruct((count, 72, PB), F32),
        grid_spec=pltpu.PrefetchScalarGridSpec(
            num_scalar_prefetch=1,
            grid=(count // 4,),
            in_specs=[single()] * 2
            + [block(q) for q in range(4)]
            + [whole(samples), whole(pt), whole(targets)],
            out_specs=pl.BlockSpec((4, 72, PB), lambda i, o: (i, 0, 0)),
        ),
        compiler_params=vmem(),
        cost_estimate=pl.CostEstimate(flops=count * 2 * 10**8, bytes_accessed=6 << 20, transcendentals=2 << 20),
        name="gram",
    )(ids, log_scale, lengthscale, points, points, points, points, samples, pt, targets)


def invert_block(block, store):
    groups = [block[8 * v : 8 * v + 8, :] for v in range(16)]
    lane = lax.broadcasted_iota(jnp.int32, (8, 128), 1)
    pivots = jnp.ones((8, 128), F32)
    spread = lambda a: jnp.broadcast_to(a, (8, 128))
    for g in range(16):
        j = 8 * g
        inside = (lane >= j) & (lane < j + 8)
        local = [spread(groups[g][:, j + b : j + b + 1]) for b in range(8)]
        p = [[spread(local[b][a : a + 1, :]) for b in range(a + 1)] for a in range(8)]
        cols = [[spread(groups[u][:, j + b : j + b + 1]) for b in range(8)] for u in range(g + 1, 16)]
        r = [
            jnp.where(inside, jnp.where(lane == j + a, 1.0, 0.0), spread(groups[g][a : a + 1, :]))
            for a in range(8)
        ]
        inv = []
        low = [[None] * 8 for _ in range(8)]
        for m in range(8):
            d = p[m][m]
            inv.append(1.0 / d)
            store(j + m, r[m] * lax.rsqrt(d))
            pivots = jnp.where(lane == j + m, d, pivots)
            for a in range(m + 1, 8):
                low[a][m] = p[a][m] * inv[m]
                r[a] = r[a] - low[a][m] * r[m]
                for b in range(m + 1, a):
                    p[a][b] = p[a][b] - low[a][m] * p[b][m]
                p[a][a] = p[a][a] - (p[a][m] * p[a][m]) * inv[m]
        q = [r[a] * inv[a] for a in range(8)]
        for b in range(7, 0, -1):
            for a in range(b):
                q[a] = q[a] - low[b][a] * q[b]
        for u in range(g + 1, 16):
            c = cols[u - g - 1]
            base = jnp.where(inside, 0.0, groups[u])
            for b in range(7, -1, -1):
                base = base - c[b] * q[b]
            groups[u] = base
    return pivots


def inverse_of(block, piece):
    def store(r, line):
        piece[r : r + 1, :] = line[:1, :]

    pivots = invert_block(block, store)
    row = lax.broadcasted_iota(jnp.int32, (128, 128), 0)
    lower = row >= lax.broadcasted_iota(jnp.int32, (128, 128), 1)
    return jnp.where(lower, piece[...], 0.0), jnp.log(pivots)


def factor_first_kernel(
    ids_ref, log_ref_in, length_ref, noise_ref, panel_ref, mine_ref, other_ref, inverse_ref, log_ref, left_ref, right_ref, work, piece
):
    i2, offset = scales(log_ref_in, length_ref)
    over = 1.0 / noise_ref[...]
    first = ids_ref[32] % 2 == 0
    for s in range(4):
        place = (s + 8 - ids_ref[33]) % 4
        mine, other = mine_ref[place], other_ref[place]
        share = jnp.concatenate([jnp.where(first, mine, other), jnp.where(first, other, mine)], axis=0)
        wide, slim = 64 * (8 - s), 64 * (s + 1)
        work[wide - 64 : wide, :wide] = share[:, :wide]
        work[slim - 64 : slim, :slim] = share[:, wide : wide + slim]
        if wide < PB:
            work[wide - 64 : wide, wide:] = jnp.zeros((64, PB - wide), F32)
        work[slim - 64 : slim, slim:] = jnp.zeros((64, PB - slim), F32)
        cross = share[:, PB:].T
        right_ref[:, slim - 64 : slim] = cross[64:65, :] * over
        right_ref[:, wide - 64 : wide] = cross[65:66, :] * over
    half = half_norm(panel_ref[...])
    left = widen(panel_ref[...], half + offset, True)
    right = widen(panel_ref[...], half, False)
    kern = jnp.exp2(i2 * lax.dot_general(left, right, NT, preferred_element_type=F32))
    row = lax.broadcasted_iota(jnp.int32, (PB, PB), 0)
    col = lax.broadcasted_iota(jnp.int32, (PB, PB), 1)
    lower = work[...]
    top = jnp.where(row >= col, lower, lower.T)
    work[...] = kern + jnp.where(row == col, JITTER, 0.0) + top * over
    t, logs = inverse_of(work[:128, :128], piece)
    rest = jnp.dot(t, work[:128, 128:], preferred_element_type=F32, precision=HI)
    u = jnp.concatenate([t, rest], axis=1)
    inverse_ref[...] = jnp.where(lax.broadcasted_iota(jnp.int32, (128, PB), 1) < 128, u, 0.0)
    away = lax.dot_general(rest, u, TN, preferred_element_type=F32, precision=HI)
    column = lax.broadcasted_iota(jnp.int32, (PB - 128, PB), 1)
    left_ref[...] = jnp.where(column < 128, 0.0, work[128:, :]) - away
    log_ref[...] = jnp.sum(logs[:1, :], axis=1, keepdims=True)


def factor_middle_kernel(work_ref, inverse_ref, log_ref, left_ref, piece):
    t, logs = inverse_of(work_ref[:128, 128:256], piece)
    rest = jnp.dot(t, work_ref[:128, :], preferred_element_type=F32, precision=HI)
    u = jnp.concatenate([rest[:, :128], t, rest[:, 256:]], axis=1)
    inverse_ref[...] = jnp.where(lax.broadcasted_iota(jnp.int32, (128, PB), 1) < 256, u, 0.0)
    away = lax.dot_general(u[:, 256:], u, TN, preferred_element_type=F32, precision=HI)
    column = lax.broadcasted_iota(jnp.int32, (PB - 256, PB), 1)
    left_ref[...] = jnp.where((column >= 128) & (column < 256), 0.0, work_ref[128:, :]) - away
    log_ref[...] = jnp.sum(logs[:1, :], axis=1, keepdims=True)


def factor_last_kernel(work_ref, inverse_ref, log_ref, work, across_ref, piece):
    done = PB - work.shape[0]
    work[...] = work_ref[...]
    row = done + lax.broadcasted_iota(jnp.int32, work.shape, 0)
    column = lax.broadcasted_iota(jnp.int32, work.shape, 1)

    def one(k, total):
        lo = pl.multiple_of(128 * k, 128)
        rows = pl.ds(pl.multiple_of(128 * k - done, 128), 128)
        t, logs = inverse_of(work[rows, pl.ds(lo, 128)], piece)
        across_ref[...] = jnp.dot(t, work[rows, :], preferred_element_type=F32, precision=HI)
        across_ref[:, pl.ds(lo, 128)] = t
        u = across_ref[...]
        inverse_ref[rows, :] = jnp.where(column[:128] < lo + 128, u, 0.0)
        away = lax.dot_general(u[:, done:], u, TN, preferred_element_type=F32, precision=HI)
        inside = (column >= lo) & (column < lo + 128)
        left = jnp.where(inside, 0.0, work[...]) - away
        work[...] = jnp.where(row >= lo + 128, left, work[...])
        return total + logs

    total = lax.fori_loop(done // 128, PB // 128, one, jnp.zeros((8, 128), F32))
    log_ref[...] = jnp.sum(total[:1, :], axis=1, keepdims=True)


def factor_first(ids, log_scale, lengthscale, noise_var, panel, mine, other):
    full = pl.BlockSpec(memory_space=pltpu.VMEM)
    smem = pl.BlockSpec(memory_space=pltpu.SMEM)
    return pl.pallas_call(
        factor_first_kernel,
        out_shape=(
            jax.ShapeDtypeStruct((128, PB), F32),
            jax.ShapeDtypeStruct((1, 1), F32),
            jax.ShapeDtypeStruct((PB - 128, PB), F32),
            jax.ShapeDtypeStruct((1, PB), F32),
        ),
        in_specs=[smem] + [full] * 6,
        out_specs=(full,) * 4,
        scratch_shapes=[pltpu.VMEM((PB, PB), F32), pltpu.VMEM((128, 128), F32)],
        compiler_params=vmem(),
        cost_estimate=pl.CostEstimate(flops=6 * 10**9, bytes_accessed=2 << 20, transcendentals=1 << 18),
        name="factor_first",
    )(ids, log_scale, lengthscale, noise_var, panel, mine, other)


def factor_middle(work):
    full = pl.BlockSpec(memory_space=pltpu.VMEM)
    return pl.pallas_call(
        factor_middle_kernel,
        out_shape=(
            jax.ShapeDtypeStruct((128, PB), F32),
            jax.ShapeDtypeStruct((1, 1), F32),
            jax.ShapeDtypeStruct((PB - 256, PB), F32),
        ),
        in_specs=[full],
        out_specs=(full,) * 3,
        scratch_shapes=[pltpu.VMEM((128, 128), F32)],
        compiler_params=vmem(),
        cost_estimate=pl.CostEstimate(flops=5 * 10**9, bytes_accessed=2 << 20, transcendentals=1 << 18),
        name="factor_middle",
    )(work)


def factor_last(work):
    full = pl.BlockSpec(memory_space=pltpu.VMEM)
    return pl.pallas_call(
        factor_last_kernel,
        out_shape=(jax.ShapeDtypeStruct(work.shape, F32), jax.ShapeDtypeStruct((1, 1), F32)),
        in_specs=[full],
        out_specs=(full, full),
        scratch_shapes=[pltpu.VMEM(work.shape, F32), pltpu.VMEM((128, PB), F32), pltpu.VMEM((128, 128), F32)],
        compiler_params=vmem(),
        cost_estimate=pl.CostEstimate(flops=10 * 10**9, bytes_accessed=2 << 20, transcendentals=1 << 18),
        name="factor_last",
    )(work)


def finish_kernel(ids_ref, log_ref, length_ref, noise_ref, own_ref, panel_ref, right_ref, *rest):
    inverse_refs, parts, (pf_ref, rhs_ref, sol_ref) = rest[:3], rest[3:-3], rest[-3:]
    i2, offset = scales(log_ref, length_ref)
    over = 1.0 / noise_ref[...]
    rows = own_ref.shape[0]
    left = widen(own_ref[...], half_norm(own_ref[...]) + offset, True)
    right = widen(panel_ref[...], half_norm(panel_ref[...]), False)
    kern = jnp.exp2(i2 * lax.dot_general(left, right, NT, preferred_element_type=F32))
    row = ids_ref[34] + lax.broadcasted_iota(jnp.int32, (rows, PB), 0)
    col = lax.broadcasted_iota(jnp.int32, (rows, PB), 1)
    a, b, c, d = (p[...] for p in parts)
    sums = (a + b) + (c + d)
    system = kern + jnp.where(row == col, JITTER, 0.0) + sums[:rows, :] * over
    both = jnp.concatenate([system, jnp.broadcast_to(right_ref[...], (8, PB))], axis=0)
    inverse = jnp.concatenate([r[...] for r in inverse_refs], axis=0)
    solved = lax.dot_general(both, inverse, NT, preferred_element_type=F32, precision=HI)
    pf = solved[:rows, :]
    sol = solved[rows:, :]
    pf_ref[...] = pf
    sol_ref[...] = sol[:1, :]
    back = lax.dot_general(sol, pf, NT, preferred_element_type=F32, precision=HI)
    rhs_ref[...] = sums[rows : rows + 1, :rows] * over - back[:1, :]


def finish(ids, log_scale, lengthscale, noise_var, inducing, panel, *others):
    rows = inducing.shape[0] // SHARDS
    full = lambda a: pl.BlockSpec(a.shape, lambda i, d: (0,) * a.ndim)
    return pl.pallas_call(
        finish_kernel,
        out_shape=(
            jax.ShapeDtypeStruct((rows, PB), F32),
            jax.ShapeDtypeStruct((1, rows), F32),
            jax.ShapeDtypeStruct((1, PB), F32),
        ),
        grid_spec=pltpu.PrefetchScalarGridSpec(
            num_scalar_prefetch=1,
            grid=(1,),
            in_specs=[single()] * 3 + [pl.BlockSpec((rows, 128), lambda i, d: (d[32], 0))]
            + [full(a) for a in (panel,) + others],
            out_specs=(
                pl.BlockSpec((rows, PB), lambda i, d: (0, 0)),
                pl.BlockSpec((1, rows), lambda i, d: (0, 0)),
                pl.BlockSpec((1, PB), lambda i, d: (0, 0)),
            ),
        ),
        compiler_params=vmem(),
        cost_estimate=pl.CostEstimate(flops=10**9, bytes_accessed=2 << 20, transcendentals=1 << 16),
        name="finish",
    )(ids, log_scale, lengthscale, noise_var, inducing, panel, *others)


def moved(x, axis, pairs):
    return lax.ppermute(x, axis, pairs)


def across(x, to):
    return lax.ppermute(x, "dp", [(i, to(i)) for i in range(SHARDS)])


def other_core(i):
    return i ^ 1


def along_x(i, k):
    return (i // 8) * 8 + (i + 2 * k) % 8


def along_y(i, k):
    return (i + 8 * k) % SHARDS


def gray(v):
    return v ^ (v >> 1)


def place_of(i):
    return i % 2, gray((i // 2) % 4), gray(i // 8)


def device_at(c, gx, gy):
    return gray(gy) * 8 + gray(gx) * 2 + c


def flipped(i, bit, which):
    c, gx, gy = place_of(i)
    return device_at(c, gx ^ (bit * (which >> 1)), gy ^ (bit * (which & 1)))


def device_numbers(shard, layer, row):
    n = jnp.arange(40, dtype=jnp.int32)
    r = n & 31
    c, gx, gy = place_of(shard)
    gx = gx ^ (((r >> 3) & 1) | (((r >> 1) & 1) << 1))
    gy = gy ^ (((r >> 2) & 1) | ((r & 1) << 1))
    order = device_at(c ^ (r >> 4), gx, gy)
    return jnp.where(n < 32, order, jnp.where(n == 32, shard, jnp.where(n == 33, layer, row))).astype(jnp.int32)


def quarters(*parts):
    n = parts[0].shape[0] // 4
    return [sum(p[n * w : n * w + n] for p in parts) for w in range(4)]


def spread_blocks(sent, bit):
    return [sent[0]] + [
        across(sent[w], functools.partial(flipped, bit=bit, which=w)) for w in (3, 2, 1)
    ]


def after(x, *first):
    return lax.optimization_barrier((x,) + first)[0]


def sum_over(x, step):
    a, b, c = (across(x, functools.partial(step, k=k)) for k in (1, 2, 3))
    return (x + a) + (b + c)


def every_share(half):
    ring = lambda k: moved(half, "ind", [(i, (i - k) % LAYERS) for i in range(LAYERS)])
    return jnp.stack([half, ring(1), ring(2), ring(-1)])


def body(
    inputs, targets, row_counts, w_in, w_mid, w_out, feat_gain, inducing, log_scale, lengthscale, noise_var
):
    shard = lax.axis_index("dp").astype(jnp.int32)
    layer = lax.axis_index("ind").astype(jnp.int32)
    slots = inputs.shape[0]
    own_rows = inducing.shape[0] // SHARDS
    ids = device_numbers(shard, layer, layer * inducing.shape[0] + shard * own_rows)
    shape = (log_scale.reshape(1, 1), lengthscale.reshape(1, 1))
    noise = noise_var.reshape(1, 1)
    trow = targets.astype(F32).reshape(1, slots)
    network = (w_in, w_mid, w_out, feat_gain.reshape(1, -1))

    panel = inducing[:PB]
    far = [moved(panel, "ind", [(0, 3)]), moved(panel, "ind", [(0, 5)])]
    samples = embed(0, 2, ids, row_counts, inputs, *network)
    panel = jnp.where(layer == 3, far[0], jnp.where(layer == 5, far[1], panel))
    panel = after(panel, samples)
    near = [
        moved(panel, "ind", [(0, 1), (3, 4), (5, 6)]),
        moved(panel, "ind", [(0, 7), (3, 2)]),
    ]
    samples = embed(2, 2, ids, row_counts, after(inputs, panel), *network, before=samples)
    in_first = (layer == 1) | (layer == 4) | (layer == 6)
    in_second = (layer == 7) | (layer == 2)
    panel = jnp.where(in_first, near[0], jnp.where(in_second, near[1], panel))

    pt, half, sent = panel_top(ids, *shape, samples, panel, trow)
    half = half + across(sent, other_core)
    away = gram(ids, 16, 16, *shape, inducing, samples, pt, trow)
    got = across(after(away, half), other_core)
    half = after(half, away)
    half = sum_over(half, along_x)
    kept = gram(ids, 0, 16, *shape, inducing, samples, pt, trow)
    half = sum_over(half, along_y)
    sums = quarters(kept, got)
    parts = spread_blocks(sums, 1)
    mine = every_share(half)
    other = across(mine, other_core)
    inverse0, log0, work, right = factor_first(ids, *shape, noise, panel, mine, other)
    inverse1, log1, work = factor_middle(work)
    parts = spread_blocks(quarters(after(parts[0], work), *parts[1:]), 2)
    inverse2, log2 = factor_last(work)
    pf, rhs, sol = finish(
        ids, *shape, noise, inducing, panel, right, inverse0, inverse1, inverse2, *(p[0] for p in parts)
    )
    return pf, rhs.reshape(own_rows), sol.reshape(PB), (log0 + log1 + log2).reshape(1)


def solution(mesh):
    return jax.shard_map(
        body,
        mesh=mesh,
        in_specs=(P("dp", None), P("dp"), P(), P(), P(), P(), P(), P("ind", None), P(), P(), P()),
        out_specs=(P(("ind", "dp"), None), P(("ind", "dp")), P(), P()),
        check_vma=False,
    )
```

```python
import functools
import jax
import jax.numpy as jnp
from jax import lax
from jax.experimental import pallas as pl
from jax.experimental.pallas import tpu as pltpu
from jax.sharding import PartitionSpec as P


PB = 512
JITTER = 0.0001
SHARDS, LAYERS = 32, 8
LOG2E = 1.4426950408889634
MASKED = -1.0e6
F32, BF16 = jnp.float32, jnp.bfloat16
HI = lax.Precision.HIGHEST
NT = (((1,), (1,)), ((), ()))
TN = (((0,), (0,)), ((), ()))


def vmem(limit=60 << 20):
    return pltpu.CompilerParams(vmem_limit_bytes=limit)


def scales(log_ref, length_ref):
    square = length_ref[...] * length_ref[...]
    return LOG2E / square, log_ref[...] * square


def single():
    return pl.BlockSpec((1, 1), lambda *at: (0, 0))


def widen(points, half, first):
    rows = points.shape[0]
    high = half.astype(BF16)
    rest = half - high.astype(F32)
    mid = rest.astype(BF16)
    low = (rest - mid.astype(F32)).astype(BF16)
    lane = lax.broadcasted_iota(jnp.int32, (rows, 128), 1)
    at = 0 if first else 3
    one = 3 if first else 0
    tail = jnp.where((lane >= one) & (lane < one + 3), 1.0, 0.0)
    tail = jnp.where(lane == at, high.astype(F32), tail)
    tail = jnp.where(lane == at + 1, mid.astype(F32), tail)
    tail = jnp.where(lane == at + 2, low.astype(F32), tail)
    return jnp.concatenate([points, tail.astype(BF16)], axis=1)


def half_norm(points):
    wide = points.astype(F32)
    return -0.5 * jnp.sum(wide * wide, axis=1, keepdims=True)


def gelu(x):
    inner = x * (0.7978845608028654 + 0.035677408136300125 * (x * x))
    half = 0.5 * x
    return half + half * jnp.tanh(inner)


def embed_kernel(base, ids_ref, counts_ref, x_ref, w1_ref, w2_ref, w3_ref, gain_ref, *rest):
    out_ref = rest[-1]
    rows = x_ref.shape[0]
    one = gelu(jnp.dot(x_ref[...], w1_ref[...], preferred_element_type=F32)).astype(BF16)
    two = gelu(jnp.dot(one, w2_ref[...], preferred_element_type=F32)).astype(BF16)
    proj = jnp.dot(two, w3_ref[...], preferred_element_type=F32)
    mean = jnp.mean(proj * proj, axis=1, keepdims=True)
    points = (proj * lax.rsqrt(mean + 1e-06) * gain_ref[...]).astype(BF16)
    index = (base + pl.program_id(0)) * rows + lax.broadcasted_iota(jnp.int32, (rows, 1), 0)
    half = jnp.where(index < counts_ref[ids_ref[32]], half_norm(points), MASKED)
    out_ref[...] = widen(points, half, False)


def embed(base, steps, ids, counts, inputs, w_in, w_mid, w_out, gain, before=None, tile=512):
    slots = inputs.shape[0]
    whole = lambda a: pl.BlockSpec(a.shape, lambda i: (0, 0), pipeline_mode=pl.Buffered(1))
    smem = pl.BlockSpec(memory_space=pltpu.SMEM)
    more = () if before is None else (before,)
    return pl.pallas_call(
        functools.partial(embed_kernel, base),
        out_shape=jax.ShapeDtypeStruct((slots, 256), BF16),
        grid=(steps,),
        in_specs=[
            smem,
            smem,
            pl.BlockSpec((tile, inputs.shape[1]), lambda i: (i + base, 0)),
            whole(w_in),
            whole(w_mid),
            whole(w_out),
            whole(gain),
        ]
        + [pl.BlockSpec(memory_space=pl.ANY)] * len(more),
        out_specs=pl.BlockSpec((tile, 256), lambda i: (i + base, 0)),
        input_output_aliases={7: 0} if more else {},
        compiler_params=vmem(),
        cost_estimate=pl.CostEstimate(
            flops=steps * 15 * 10**8, bytes_accessed=4 << 20, transcendentals=steps << 20
        ),
        name="embed",
    )(ids, counts, inputs, w_in, w_mid, w_out, gain, *more)


WIDE = PB + 128


def panel_kernel(
    ids_ref, log_ref, length_ref, samples_ref, panel_ref, t_ref, pt_ref, kept_ref, sent_ref, total, crossed
):
    step = pl.program_id(0)
    i2, offset = scales(log_ref, length_ref)
    share = ids_ref[33] % 4
    samples = samples_ref[...]
    panel = widen(panel_ref[...], half_norm(panel_ref[...]) + offset, True)
    mine = jnp.concatenate(
        [
            panel_ref[pl.ds(pl.multiple_of(share * 64, 64), 64), :],
            panel_ref[pl.ds(pl.multiple_of((7 - share) * 64, 64), 64), :],
        ],
        axis=0,
    )
    chunk = widen(mine, half_norm(mine) + offset, True)
    kern = jnp.exp2(i2 * lax.dot_general(samples, panel, NT, preferred_element_type=F32)).astype(BF16)
    part = jnp.exp2(i2 * lax.dot_general(chunk, samples, NT, preferred_element_type=F32)).astype(BF16)
    pt_ref[...] = kern
    sums = jnp.dot(part, kern, preferred_element_type=F32)
    cross = jnp.sum(part.astype(F32) * t_ref[...], axis=1, keepdims=True)
    cross = jnp.broadcast_to(cross, (128, 128))

    @pl.when(step == 0)
    def _():
        total[...] = sums
        crossed[...] = cross

    @pl.when(step > 0)
    def _():
        total[...] += sums
        crossed[...] += cross

    for s in range(4):

        @pl.when((step == pl.num_programs(0) - 1) & (share == s))
        def _(s=s):
            packed = jnp.concatenate(
                [
                    total[64:, : 64 * (8 - s)],
                    total[:64, : 64 * (s + 1)],
                    crossed[:64, :1],
                    crossed[64:, :1],
                    jnp.zeros((64, 62), F32),
                ],
                axis=1,
            )
            first = ids_ref[32] % 2 == 0
            kept_ref[...] = jnp.where(first, packed[:32, :], packed[32:, :])
            sent_ref[...] = jnp.where(first, packed[32:, :], packed[:32, :])


def panel_top(ids, log_scale, lengthscale, samples, panel, targets, tile=512):
    slots = samples.shape[0]
    smem = pl.BlockSpec(memory_space=pltpu.SMEM)
    return pl.pallas_call(
        panel_kernel,
        out_shape=(
            jax.ShapeDtypeStruct((slots, PB), BF16),
            jax.ShapeDtypeStruct((32, WIDE), F32),
            jax.ShapeDtypeStruct((32, WIDE), F32),
        ),
        grid=(slots // tile,),
        in_specs=[
            smem,
            single(),
            single(),
            pl.BlockSpec((tile, 256), lambda i: (i, 0)),
            pl.BlockSpec(panel.shape, lambda i: (0, 0)),
            pl.BlockSpec((1, tile), lambda i: (0, i)),
        ],
        out_specs=(
            pl.BlockSpec((tile, PB), lambda i: (i, 0)),
            pl.BlockSpec((32, WIDE), lambda i: (0, 0)),
            pl.BlockSpec((32, WIDE), lambda i: (0, 0)),
        ),
        scratch_shapes=[pltpu.VMEM((128, PB), F32), pltpu.VMEM((128, 128), F32)],
        compiler_params=vmem(36 << 20),
        cost_estimate=pl.CostEstimate(flops=15 * 10**8, bytes_accessed=4 << 20, transcendentals=1 << 20),
        name="panel",
    )(ids, log_scale, lengthscale, samples, panel, targets)


def gram_kernel(ids_ref, log_ref, length_ref, *refs):
    points_refs, (samples_ref, pt_ref, t_ref, out_ref) = refs[:4], refs[4:]
    i2, offset = scales(log_ref, length_ref)
    raw = jnp.concatenate([p[...] for p in points_refs], axis=0)
    points = widen(raw, half_norm(raw) + offset, True)
    kern = jnp.exp2(
        i2 * lax.dot_general(points, samples_ref[...], NT, preferred_element_type=F32)
    ).astype(BF16)
    crossed = jnp.sum(kern.astype(F32) * t_ref[...], axis=1, keepdims=True)
    crossed = jnp.broadcast_to(crossed, (256, 128)).T
    sums = jnp.dot(kern, pt_ref[...], preferred_element_type=F32)
    for b in range(4):
        out_ref[b, :64, :] = sums[b * 64 : b * 64 + 64, :]
        out_ref[b, 64:, :] = jnp.concatenate(
            [crossed[:8, b * 64 : b * 64 + 64], jnp.zeros((8, PB - 64), F32)], axis=1
        )


def gram(ids, at, count, log_scale, lengthscale, points, samples, pt, targets):
    whole = lambda a: pl.BlockSpec(a.shape, lambda i, o: (0, 0), pipeline_mode=pl.Buffered(1))
    block = lambda q: pl.BlockSpec((64, 128), lambda i, o: (o[at + 4 * i + q], 0))
    return pl.pallas_call(
        gram_kernel,
        out_shape=jax.ShapeDtypeStruct((count, 72, PB), F32),
        grid_spec=pltpu.PrefetchScalarGridSpec(
            num_scalar_prefetch=1,
            grid=(count // 4,),
            in_specs=[single()] * 2
            + [block(q) for q in range(4)]
            + [whole(samples), whole(pt), whole(targets)],
            out_specs=pl.BlockSpec((4, 72, PB), lambda i, o: (i, 0, 0)),
        ),
        compiler_params=vmem(36 << 20),
        cost_estimate=pl.CostEstimate(flops=count * 2 * 10**8, bytes_accessed=6 << 20, transcendentals=2 << 20),
        name="gram",
    )(ids, log_scale, lengthscale, points, points, points, points, samples, pt, targets)


def invert_block(block, store):
    groups = [block[8 * v : 8 * v + 8, :] for v in range(16)]
    lane = lax.broadcasted_iota(jnp.int32, (8, 128), 1)
    pivots = jnp.ones((8, 128), F32)
    spread = lambda a: jnp.broadcast_to(a, (8, 128))
    for g in range(16):
        j = 8 * g
        inside = (lane >= j) & (lane < j + 8)
        local = [spread(groups[g][:, j + b : j + b + 1]) for b in range(8)]
        p = [[spread(local[b][a : a + 1, :]) for b in range(a + 1)] for a in range(8)]
        cols = [[spread(groups[u][:, j + b : j + b + 1]) for b in range(8)] for u in range(g + 1, 16)]
        r = [
            jnp.where(inside, jnp.where(lane == j + a, 1.0, 0.0), spread(groups[g][a : a + 1, :]))
            for a in range(8)
        ]
        inv = []
        low = [[None] * 8 for _ in range(8)]
        for m in range(8):
            d = p[m][m]
            inv.append(1.0 / d)
            store(j + m, r[m] * lax.rsqrt(d))
            pivots = jnp.where(lane == j + m, d, pivots)
            for a in range(m + 1, 8):
                low[a][m] = p[a][m] * inv[m]
                r[a] = r[a] - low[a][m] * r[m]
                for b in range(m + 1, a):
                    p[a][b] = p[a][b] - low[a][m] * p[b][m]
                p[a][a] = p[a][a] - (p[a][m] * p[a][m]) * inv[m]
        q = [r[a] * inv[a] for a in range(8)]
        for b in range(7, 0, -1):
            for a in range(b):
                q[a] = q[a] - low[b][a] * q[b]
        for u in range(g + 1, 16):
            c = cols[u - g - 1]
            base = jnp.where(inside, 0.0, groups[u])
            for b in range(7, -1, -1):
                base = base - c[b] * q[b]
            groups[u] = base
    return pivots


def inverse_of(block, piece):
    def store(r, line):
        piece[r : r + 1, :] = line[:1, :]

    pivots = invert_block(block, store)
    row = lax.broadcasted_iota(jnp.int32, (128, 128), 0)
    lower = row >= lax.broadcasted_iota(jnp.int32, (128, 128), 1)
    return jnp.where(lower, piece[...], 0.0), jnp.log(pivots)


def factor_first_kernel(
    ids_ref, log_ref_in, length_ref, noise_ref, panel_ref, mine_ref, other_ref, inverse_ref, log_ref, left_ref, right_ref, work, piece
):
    i2, offset = scales(log_ref_in, length_ref)
    over = 1.0 / noise_ref[...]
    first = ids_ref[32] % 2 == 0
    for s in range(4):
        place = (s + 8 - ids_ref[33]) % 4
        mine, other = mine_ref[place], other_ref[place]
        share = jnp.concatenate([jnp.where(first, mine, other), jnp.where(first, other, mine)], axis=0)
        wide, slim = 64 * (8 - s), 64 * (s + 1)
        work[wide - 64 : wide, :wide] = share[:, :wide]
        work[slim - 64 : slim, :slim] = share[:, wide : wide + slim]
        if wide < PB:
            work[wide - 64 : wide, wide:] = jnp.zeros((64, PB - wide), F32)
        work[slim - 64 : slim, slim:] = jnp.zeros((64, PB - slim), F32)
        cross = share[:, PB:].T
        right_ref[:, slim - 64 : slim] = cross[64:65, :] * over
        right_ref[:, wide - 64 : wide] = cross[65:66, :] * over
    half = half_norm(panel_ref[...])
    left = widen(panel_ref[...], half + offset, True)
    right = widen(panel_ref[...], half, False)
    kern = jnp.exp2(i2 * lax.dot_general(left, right, NT, preferred_element_type=F32))
    row = lax.broadcasted_iota(jnp.int32, (PB, PB), 0)
    col = lax.broadcasted_iota(jnp.int32, (PB, PB), 1)
    lower = work[...]
    top = jnp.where(row >= col, lower, lower.T)
    work[...] = kern + jnp.where(row == col, JITTER, 0.0) + top * over
    t, logs = inverse_of(work[:128, :128], piece)
    rest = jnp.dot(t, work[:128, 128:], preferred_element_type=F32, precision=HI)
    u = jnp.concatenate([t, rest], axis=1)
    inverse_ref[...] = jnp.where(lax.broadcasted_iota(jnp.int32, (128, PB), 1) < 128, u, 0.0)
    away = lax.dot_general(rest, u, TN, preferred_element_type=F32, precision=HI)
    column = lax.broadcasted_iota(jnp.int32, (PB - 128, PB), 1)
    left_ref[...] = jnp.where(column < 128, 0.0, work[128:, :]) - away
    log_ref[...] = jnp.sum(logs[:1, :], axis=1, keepdims=True)


def factor_middle_kernel(work_ref, inverse_ref, log_ref, left_ref, piece):
    t, logs = inverse_of(work_ref[:128, 128:256], piece)
    rest = jnp.dot(t, work_ref[:128, :], preferred_element_type=F32, precision=HI)
    u = jnp.concatenate([rest[:, :128], t, rest[:, 256:]], axis=1)
    inverse_ref[...] = jnp.where(lax.broadcasted_iota(jnp.int32, (128, PB), 1) < 256, u, 0.0)
    away = lax.dot_general(u[:, 256:], u, TN, preferred_element_type=F32, precision=HI)
    column = lax.broadcasted_iota(jnp.int32, (PB - 256, PB), 1)
    left_ref[...] = jnp.where((column >= 128) & (column < 256), 0.0, work_ref[128:, :]) - away
    log_ref[...] = jnp.sum(logs[:1, :], axis=1, keepdims=True)


def factor_last_kernel(work_ref, inverse_ref, log_ref, work, across_ref, piece):
    done = PB - work.shape[0]
    work[...] = work_ref[...]
    row = done + lax.broadcasted_iota(jnp.int32, work.shape, 0)
    column = lax.broadcasted_iota(jnp.int32, work.shape, 1)

    def one(k, total):
        lo = pl.multiple_of(128 * k, 128)
        rows = pl.ds(pl.multiple_of(128 * k - done, 128), 128)
        t, logs = inverse_of(work[rows, pl.ds(lo, 128)], piece)
        across_ref[...] = jnp.dot(t, work[rows, :], preferred_element_type=F32, precision=HI)
        across_ref[:, pl.ds(lo, 128)] = t
        u = across_ref[...]
        inverse_ref[rows, :] = jnp.where(column[:128] < lo + 128, u, 0.0)
        away = lax.dot_general(u[:, done:], u, TN, preferred_element_type=F32, precision=HI)
        inside = (column >= lo) & (column < lo + 128)
        left = jnp.where(inside, 0.0, work[...]) - away
        work[...] = jnp.where(row >= lo + 128, left, work[...])
        return total + logs

    total = lax.fori_loop(done // 128, PB // 128, one, jnp.zeros((8, 128), F32))
    log_ref[...] = jnp.sum(total[:1, :], axis=1, keepdims=True)


def factor_first(ids, log_scale, lengthscale, noise_var, panel, mine, other):
    full = pl.BlockSpec(memory_space=pltpu.VMEM)
    smem = pl.BlockSpec(memory_space=pltpu.SMEM)
    return pl.pallas_call(
        factor_first_kernel,
        out_shape=(
            jax.ShapeDtypeStruct((128, PB), F32),
            jax.ShapeDtypeStruct((1, 1), F32),
            jax.ShapeDtypeStruct((PB - 128, PB), F32),
            jax.ShapeDtypeStruct((1, PB), F32),
        ),
        in_specs=[smem] + [full] * 6,
        out_specs=(full,) * 4,
        scratch_shapes=[pltpu.VMEM((PB, PB), F32), pltpu.VMEM((128, 128), F32)],
        compiler_params=vmem(20 << 20),
        cost_estimate=pl.CostEstimate(flops=6 * 10**9, bytes_accessed=2 << 20, transcendentals=1 << 18),
        name="factor_first",
    )(ids, log_scale, lengthscale, noise_var, panel, mine, other)


def factor_middle(work):
    full = pl.BlockSpec(memory_space=pltpu.VMEM)
    return pl.pallas_call(
        factor_middle_kernel,
        out_shape=(
            jax.ShapeDtypeStruct((128, PB), F32),
            jax.ShapeDtypeStruct((1, 1), F32),
            jax.ShapeDtypeStruct((PB - 256, PB), F32),
        ),
        in_specs=[full],
        out_specs=(full,) * 3,
        scratch_shapes=[pltpu.VMEM((128, 128), F32)],
        compiler_params=vmem(20 << 20),
        cost_estimate=pl.CostEstimate(flops=5 * 10**9, bytes_accessed=2 << 20, transcendentals=1 << 18),
        name="factor_middle",
    )(work)


def factor_last(work):
    full = pl.BlockSpec(memory_space=pltpu.VMEM)
    return pl.pallas_call(
        factor_last_kernel,
        out_shape=(jax.ShapeDtypeStruct(work.shape, F32), jax.ShapeDtypeStruct((1, 1), F32)),
        in_specs=[full],
        out_specs=(full, full),
        scratch_shapes=[pltpu.VMEM(work.shape, F32), pltpu.VMEM((128, PB), F32), pltpu.VMEM((128, 128), F32)],
        compiler_params=vmem(20 << 20),
        cost_estimate=pl.CostEstimate(flops=10 * 10**9, bytes_accessed=2 << 20, transcendentals=1 << 18),
        name="factor_last",
    )(work)


def finish_kernel(ids_ref, log_ref, length_ref, noise_ref, own_ref, panel_ref, right_ref, *rest):
    inverse_refs, log_refs, parts = rest[:3], rest[3:6], rest[6:-4]
    pf_ref, rhs_ref, sol_ref, det_ref = rest[-4:]
    det_ref[...] = log_refs[0][...] + log_refs[1][...] + log_refs[2][...]
    i2, offset = scales(log_ref, length_ref)
    over = 1.0 / noise_ref[...]
    rows = own_ref.shape[0]
    left = widen(own_ref[...], half_norm(own_ref[...]) + offset, True)
    right = widen(panel_ref[...], half_norm(panel_ref[...]), False)
    kern = jnp.exp2(i2 * lax.dot_general(left, right, NT, preferred_element_type=F32))
    row = ids_ref[34] + lax.broadcasted_iota(jnp.int32, (rows, PB), 0)
    col = lax.broadcasted_iota(jnp.int32, (rows, PB), 1)
    a, b, c, d = (p[...] for p in parts)
    sums = (a + b) + (c + d)
    system = kern + jnp.where(row == col, JITTER, 0.0) + sums[:rows, :] * over
    both = jnp.concatenate([system, jnp.broadcast_to(right_ref[...], (8, PB))], axis=0)
    inverse = jnp.concatenate([r[...] for r in inverse_refs], axis=0)
    solved = lax.dot_general(both, inverse, NT, preferred_element_type=F32, precision=HI)
    pf = solved[:rows, :]
    sol = solved[rows:, :]
    pf_ref[...] = pf
    sol_ref[...] = sol[:1, :]
    back = lax.dot_general(sol, pf, NT, preferred_element_type=F32, precision=HI)
    rhs_ref[...] = sums[rows : rows + 1, :rows] * over - back[:1, :]


def finish(ids, log_scale, lengthscale, noise_var, inducing, panel, *others):
    rows = inducing.shape[0] // SHARDS
    full = lambda a: pl.BlockSpec(a.shape, lambda i, d: (0,) * a.ndim)
    return pl.pallas_call(
        finish_kernel,
        out_shape=(
            jax.ShapeDtypeStruct((rows, PB), F32),
            jax.ShapeDtypeStruct((1, rows), F32),
            jax.ShapeDtypeStruct((1, PB), F32),
            jax.ShapeDtypeStruct((1, 1), F32),
        ),
        grid_spec=pltpu.PrefetchScalarGridSpec(
            num_scalar_prefetch=1,
            grid=(1,),
            in_specs=[single()] * 3 + [pl.BlockSpec((rows, 128), lambda i, d: (d[32], 0))]
            + [full(a) for a in (panel,) + others],
            out_specs=(
                pl.BlockSpec((rows, PB), lambda i, d: (0, 0)),
                pl.BlockSpec((1, rows), lambda i, d: (0, 0)),
                pl.BlockSpec((1, PB), lambda i, d: (0, 0)),
                single(),
            ),
        ),
        compiler_params=vmem(20 << 20),
        cost_estimate=pl.CostEstimate(flops=10**9, bytes_accessed=2 << 20, transcendentals=1 << 16),
        name="finish",
    )(ids, log_scale, lengthscale, noise_var, inducing, panel, *others)


def moved(x, axis, pairs):
    return lax.ppermute(x, axis, pairs)


def across(x, to):
    return lax.ppermute(x, "dp", [(i, to(i)) for i in range(SHARDS)])


def other_core(i):
    return i ^ 1


def along_x(i, k):
    return (i // 8) * 8 + (i + 2 * k) % 8


def along_y(i, k):
    return (i + 8 * k) % SHARDS


def gray(v):
    return v ^ (v >> 1)


def place_of(i):
    return i % 2, gray((i // 2) % 4), gray(i // 8)


def device_at(c, gx, gy):
    return gray(gy) * 8 + gray(gx) * 2 + c


def flipped(i, bit, which):
    c, gx, gy = place_of(i)
    return device_at(c, gx ^ (bit * (which >> 1)), gy ^ (bit * (which & 1)))


def device_numbers(shard, layer, row):
    n = jnp.arange(40, dtype=jnp.int32)
    r = n & 31
    c, gx, gy = place_of(shard)
    gx = gx ^ (((r >> 3) & 1) | (((r >> 1) & 1) << 1))
    gy = gy ^ (((r >> 2) & 1) | ((r & 1) << 1))
    order = device_at(c ^ (r >> 4), gx, gy)
    return jnp.where(n < 32, order, jnp.where(n == 32, shard, jnp.where(n == 33, layer, row))).astype(jnp.int32)


def quarters(*parts):
    n = parts[0].shape[0] // 4
    return [sum(p[n * w : n * w + n] for p in parts) for w in range(4)]


def spread_blocks(sent, bit):
    return [sent[0]] + [
        across(sent[w], functools.partial(flipped, bit=bit, which=w)) for w in (3, 2, 1)
    ]


def after(x, *first):
    return lax.optimization_barrier((x,) + first)[0]


def sum_over(x, step):
    a, b, c = (across(x, functools.partial(step, k=k)) for k in (1, 2, 3))
    return (x + a) + (b + c)


def every_share(half):
    ring = lambda k: moved(half, "ind", [(i, (i - k) % LAYERS) for i in range(LAYERS)])
    shares = [half, ring(1), ring(2), ring(-1)]
    return jnp.stack(shares)


def body(
    inputs, targets, row_counts, w_in, w_mid, w_out, feat_gain, inducing, log_scale, lengthscale, noise_var
):
    shard = lax.axis_index("dp").astype(jnp.int32)
    layer = lax.axis_index("ind").astype(jnp.int32)
    slots = inputs.shape[0]
    own_rows = inducing.shape[0] // SHARDS
    ids = device_numbers(shard, layer, layer * inducing.shape[0] + shard * own_rows)
    shape = (log_scale.reshape(1, 1), lengthscale.reshape(1, 1))
    noise = noise_var.reshape(1, 1)
    trow = targets.astype(F32).reshape(1, slots)
    network = (w_in, w_mid, w_out, feat_gain.reshape(1, -1))

    panel = inducing[:PB]
    far = [moved(panel, "ind", [(0, 3)]), moved(panel, "ind", [(0, 5)])]
    samples = embed(0, 2, ids, row_counts, inputs, *network)
    panel = jnp.where(layer == 3, far[0], jnp.where(layer == 5, far[1], panel))
    panel = after(panel, samples)
    near = [
        moved(panel, "ind", [(0, 1), (3, 4), (5, 6)]),
        moved(panel, "ind", [(0, 7), (3, 2)]),
    ]
    samples = embed(2, 2, ids, row_counts, after(inputs, panel), *network, before=samples)
    in_first = (layer == 1) | (layer == 4) | (layer == 6)
    in_second = (layer == 7) | (layer == 2)
    panel = jnp.where(in_first, near[0], jnp.where(in_second, near[1], panel))

    pt, half, sent = panel_top(ids, *shape, samples, panel, trow)
    half = half + across(sent, other_core)
    away = gram(ids, 16, 16, *shape, inducing, samples, pt, trow)
    got = across(after(away, half), other_core)
    half = after(half, away)
    half = sum_over(half, along_x)
    kept = gram(ids, 0, 16, *shape, inducing, samples, pt, trow)
    half = sum_over(half, along_y)
    sums = quarters(kept, got)
    parts = spread_blocks(sums, 1)
    mine = every_share(half)
    other = across(mine, other_core)
    inverse0, log0, work, right = factor_first(ids, *shape, noise, panel, mine, other)
    inverse1, log1, work = factor_middle(work)
    parts = spread_blocks(quarters(after(parts[0], work), *parts[1:]), 2)
    inverse2, log2 = factor_last(work)
    pf, rhs, sol, det = finish(
        ids, *shape, noise, inducing, panel, right, inverse0, inverse1, inverse2, log0, log1, log2, *(p[0] for p in parts)
    )
    return pf, rhs.reshape(own_rows), sol.reshape(PB), det.reshape(1)


def solution(mesh):
    return jax.shard_map(
        body,
        mesh=mesh,
        in_specs=(P("dp", None), P("dp"), P(), P(), P(), P(), P(), P("ind", None), P(), P(), P()),
        out_specs=(P(("ind", "dp"), None), P(("ind", "dp")), P(), P()),
        check_vma=False,
    )
```

```python
import functools
import jax
import jax.numpy as jnp
from jax import lax
from jax.experimental import pallas as pl
from jax.experimental.pallas import tpu as pltpu
from jax.sharding import PartitionSpec as P


PB = 512
JITTER = 0.0001
SHARDS, LAYERS = 32, 8
LOG2E = 1.4426950408889634
MASKED = -1.0e6
F32, BF16 = jnp.float32, jnp.bfloat16
HI = lax.Precision.HIGHEST
NT = (((1,), (1,)), ((), ()))
TN = (((0,), (0,)), ((), ()))


def vmem(limit=60 << 20):
    return pltpu.CompilerParams(vmem_limit_bytes=limit)


def scales(log_ref, length_ref):
    square = length_ref[...] * length_ref[...]
    return LOG2E / square, log_ref[...] * square


def single():
    return pl.BlockSpec((1, 1), lambda *at: (0, 0))


def widen(points, half, first):
    rows = points.shape[0]
    high = half.astype(BF16)
    rest = half - high.astype(F32)
    mid = rest.astype(BF16)
    low = (rest - mid.astype(F32)).astype(BF16)
    lane = lax.broadcasted_iota(jnp.int32, (rows, 128), 1)
    at = 0 if first else 3
    one = 3 if first else 0
    tail = jnp.where((lane >= one) & (lane < one + 3), 1.0, 0.0)
    tail = jnp.where(lane == at, high.astype(F32), tail)
    tail = jnp.where(lane == at + 1, mid.astype(F32), tail)
    tail = jnp.where(lane == at + 2, low.astype(F32), tail)
    return jnp.concatenate([points, tail.astype(BF16)], axis=1)


def half_norm(points):
    wide = points.astype(F32)
    return -0.5 * jnp.sum(wide * wide, axis=1, keepdims=True)


def gelu(x):
    inner = x * (0.7978845608028654 + 0.035677408136300125 * (x * x))
    half = 0.5 * x
    return half + half * jnp.tanh(inner)


def embed_kernel(base, ids_ref, counts_ref, x_ref, w1_ref, w2_ref, w3_ref, gain_ref, *rest):
    out_ref = rest[-1]
    rows = x_ref.shape[0]
    one = gelu(jnp.dot(x_ref[...], w1_ref[...], preferred_element_type=F32)).astype(BF16)
    two = gelu(jnp.dot(one, w2_ref[...], preferred_element_type=F32)).astype(BF16)
    proj = jnp.dot(two, w3_ref[...], preferred_element_type=F32)
    mean = jnp.mean(proj * proj, axis=1, keepdims=True)
    points = (proj * lax.rsqrt(mean + 1e-06) * gain_ref[...]).astype(BF16)
    index = (base + pl.program_id(0)) * rows + lax.broadcasted_iota(jnp.int32, (rows, 1), 0)
    half = jnp.where(index < counts_ref[ids_ref[32]], half_norm(points), MASKED)
    out_ref[...] = widen(points, half, False)


def embed(base, steps, ids, counts, inputs, w_in, w_mid, w_out, gain, before=None, tile=512):
    slots = inputs.shape[0]
    whole = lambda a: pl.BlockSpec(a.shape, lambda i: (0, 0), pipeline_mode=pl.Buffered(1))
    smem = pl.BlockSpec(memory_space=pltpu.SMEM)
    more = () if before is None else (before,)
    return pl.pallas_call(
        functools.partial(embed_kernel, base),
        out_shape=jax.ShapeDtypeStruct((slots, 256), BF16),
        grid=(steps,),
        in_specs=[
            smem,
            smem,
            pl.BlockSpec((tile, inputs.shape[1]), lambda i: (i + base, 0)),
            whole(w_in),
            whole(w_mid),
            whole(w_out),
            whole(gain),
        ]
        + [pl.BlockSpec(memory_space=pl.ANY)] * len(more),
        out_specs=pl.BlockSpec((tile, 256), lambda i: (i + base, 0)),
        input_output_aliases={7: 0} if more else {},
        compiler_params=vmem(),
        cost_estimate=pl.CostEstimate(
            flops=steps * 15 * 10**8, bytes_accessed=4 << 20, transcendentals=steps << 20
        ),
        name="embed",
    )(ids, counts, inputs, w_in, w_mid, w_out, gain, *more)


WIDE = PB + 128


def panel_kernel(
    ids_ref, log_ref, length_ref, samples_ref, panel_ref, t_ref, pt_ref, kept_ref, sent_ref, total, crossed
):
    step = pl.program_id(0)
    i2, offset = scales(log_ref, length_ref)
    share = ids_ref[33] % 4
    samples = samples_ref[...]
    panel = widen(panel_ref[...], half_norm(panel_ref[...]) + offset, True)
    mine = jnp.concatenate(
        [
            panel_ref[pl.ds(pl.multiple_of(share * 64, 64), 64), :],
            panel_ref[pl.ds(pl.multiple_of((7 - share) * 64, 64), 64), :],
        ],
        axis=0,
    )
    chunk = widen(mine, half_norm(mine) + offset, True)
    kern = jnp.exp2(i2 * lax.dot_general(samples, panel, NT, preferred_element_type=F32)).astype(BF16)
    part = jnp.exp2(i2 * lax.dot_general(chunk, samples, NT, preferred_element_type=F32)).astype(BF16)
    pt_ref[...] = kern
    sums = jnp.dot(part, kern, preferred_element_type=F32)
    cross = jnp.sum(part.astype(F32) * t_ref[...], axis=1, keepdims=True)
    cross = jnp.broadcast_to(cross, (128, 128))

    @pl.when(step == 0)
    def _():
        total[...] = sums
        crossed[...] = cross

    @pl.when(step > 0)
    def _():
        total[...] += sums
        crossed[...] += cross

    for s in range(4):

        @pl.when((step == pl.num_programs(0) - 1) & (share == s))
        def _(s=s):
            packed = jnp.concatenate(
                [
                    total[64:, : 64 * (8 - s)],
                    total[:64, : 64 * (s + 1)],
                    crossed[:64, :1],
                    crossed[64:, :1],
                    jnp.zeros((64, 62), F32),
                ],
                axis=1,
            )
            first = ids_ref[32] % 2 == 0
            kept_ref[...] = jnp.where(first, packed[:32, :], packed[32:, :])
            sent_ref[...] = jnp.where(first, packed[32:, :], packed[:32, :])


def panel_top(ids, log_scale, lengthscale, samples, panel, targets, tile=512):
    slots = samples.shape[0]
    smem = pl.BlockSpec(memory_space=pltpu.SMEM)
    return pl.pallas_call(
        panel_kernel,
        out_shape=(
            jax.ShapeDtypeStruct((slots, PB), BF16),
            jax.ShapeDtypeStruct((32, WIDE), F32),
            jax.ShapeDtypeStruct((32, WIDE), F32),
        ),
        grid=(slots // tile,),
        in_specs=[
            smem,
            single(),
            single(),
            pl.BlockSpec((tile, 256), lambda i: (i, 0)),
            pl.BlockSpec(panel.shape, lambda i: (0, 0)),
            pl.BlockSpec((1, tile), lambda i: (0, i)),
        ],
        out_specs=(
            pl.BlockSpec((tile, PB), lambda i: (i, 0)),
            pl.BlockSpec((32, WIDE), lambda i: (0, 0)),
            pl.BlockSpec((32, WIDE), lambda i: (0, 0)),
        ),
        scratch_shapes=[pltpu.VMEM((128, PB), F32), pltpu.VMEM((128, 128), F32)],
        compiler_params=vmem(36 << 20),
        cost_estimate=pl.CostEstimate(flops=15 * 10**8, bytes_accessed=4 << 20, transcendentals=1 << 20),
        name="panel",
    )(ids, log_scale, lengthscale, samples, panel, targets)


def gram_kernel(ids_ref, log_ref, length_ref, *refs):
    points_refs, (samples_ref, pt_ref, t_ref, out_ref) = refs[:4], refs[4:]
    i2, offset = scales(log_ref, length_ref)
    raw = jnp.concatenate([p[...] for p in points_refs], axis=0)
    points = widen(raw, half_norm(raw) + offset, True)
    kern = jnp.exp2(
        i2 * lax.dot_general(points, samples_ref[...], NT, preferred_element_type=F32)
    ).astype(BF16)
    crossed = jnp.sum(kern.astype(F32) * t_ref[...], axis=1, keepdims=True)
    crossed = jnp.broadcast_to(crossed, (256, 128)).T
    sums = jnp.dot(kern, pt_ref[...], preferred_element_type=F32)
    for b in range(4):
        out_ref[b, :64, :] = sums[b * 64 : b * 64 + 64, :]
        out_ref[b, 64:, :] = jnp.concatenate(
            [crossed[:8, b * 64 : b * 64 + 64], jnp.zeros((8, PB - 64), F32)], axis=1
        )


def gram(ids, at, count, log_scale, lengthscale, points, samples, pt, targets):
    whole = lambda a: pl.BlockSpec(a.shape, lambda i, o: (0, 0), pipeline_mode=pl.Buffered(1))
    block = lambda q: pl.BlockSpec((64, 128), lambda i, o: (o[at + 4 * i + q], 0))
    return pl.pallas_call(
        gram_kernel,
        out_shape=jax.ShapeDtypeStruct((count, 72, PB), F32),
        grid_spec=pltpu.PrefetchScalarGridSpec(
            num_scalar_prefetch=1,
            grid=(count // 4,),
            in_specs=[single()] * 2
            + [block(q) for q in range(4)]
            + [whole(samples), whole(pt), whole(targets)],
            out_specs=pl.BlockSpec((4, 72, PB), lambda i, o: (i, 0, 0)),
        ),
        compiler_params=vmem(36 << 20),
        cost_estimate=pl.CostEstimate(flops=count * 2 * 10**8, bytes_accessed=6 << 20, transcendentals=2 << 20),
        name="gram",
    )(ids, log_scale, lengthscale, points, points, points, points, samples, pt, targets)


def invert_block(block, store):
    groups = [block[8 * v : 8 * v + 8, :] for v in range(16)]
    lane = lax.broadcasted_iota(jnp.int32, (8, 128), 1)
    pivots = jnp.ones((8, 128), F32)
    spread = lambda a: jnp.broadcast_to(a, (8, 128))
    for g in range(16):
        j = 8 * g
        inside = (lane >= j) & (lane < j + 8)
        local = [spread(groups[g][:, j + b : j + b + 1]) for b in range(8)]
        p = [[spread(local[b][a : a + 1, :]) for b in range(a + 1)] for a in range(8)]
        cols = [[spread(groups[u][:, j + b : j + b + 1]) for b in range(8)] for u in range(g + 1, 16)]
        r = [
            jnp.where(inside, jnp.where(lane == j + a, 1.0, 0.0), spread(groups[g][a : a + 1, :]))
            for a in range(8)
        ]
        inv = []
        low = [[None] * 8 for _ in range(8)]
        for m in range(8):
            d = p[m][m]
            inv.append(1.0 / d)
            store(j + m, r[m] * lax.rsqrt(d))
            pivots = jnp.where(lane == j + m, d, pivots)
            for a in range(m + 1, 8):
                low[a][m] = p[a][m] * inv[m]
                r[a] = r[a] - low[a][m] * r[m]
                for b in range(m + 1, a):
                    p[a][b] = p[a][b] - low[a][m] * p[b][m]
                p[a][a] = p[a][a] - (p[a][m] * p[a][m]) * inv[m]
        q = [r[a] * inv[a] for a in range(8)]
        for b in range(7, 0, -1):
            for a in range(b):
                q[a] = q[a] - low[b][a] * q[b]
        for u in range(g + 1, 16):
            c = cols[u - g - 1]
            base = jnp.where(inside, 0.0, groups[u])
            for b in range(7, -1, -1):
                base = base - c[b] * q[b]
            groups[u] = base
    return pivots


def inverse_of(block, piece):
    def store(r, line):
        piece[r : r + 1, :] = line[:1, :]

    pivots = invert_block(block, store)
    row = lax.broadcasted_iota(jnp.int32, (128, 128), 0)
    lower = row >= lax.broadcasted_iota(jnp.int32, (128, 128), 1)
    return jnp.where(lower, piece[...], 0.0), jnp.log(pivots)


def factor_first_kernel(
    ids_ref, log_ref_in, length_ref, noise_ref, panel_ref, mine_ref, other_ref, inverse_ref, log_ref, left_ref, right_ref, work, piece
):
    i2, offset = scales(log_ref_in, length_ref)
    over = 1.0 / noise_ref[...]
    first = ids_ref[32] % 2 == 0
    for s in range(4):
        place = (s + 8 - ids_ref[33]) % 4
        mine, other = mine_ref[place], other_ref[place]
        share = jnp.concatenate([jnp.where(first, mine, other), jnp.where(first, other, mine)], axis=0)
        wide, slim = 64 * (8 - s), 64 * (s + 1)
        work[wide - 64 : wide, :wide] = share[:, :wide]
        work[slim - 64 : slim, :slim] = share[:, wide : wide + slim]
        if wide < PB:
            work[wide - 64 : wide, wide:] = jnp.zeros((64, PB - wide), F32)
        work[slim - 64 : slim, slim:] = jnp.zeros((64, PB - slim), F32)
        cross = share[:, PB:].T
        right_ref[:, slim - 64 : slim] = cross[64:65, :] * over
        right_ref[:, wide - 64 : wide] = cross[65:66, :] * over
    half = half_norm(panel_ref[...])
    left = widen(panel_ref[...], half + offset, True)
    right = widen(panel_ref[...], half, False)
    kern = jnp.exp2(i2 * lax.dot_general(left, right, NT, preferred_element_type=F32))
    row = lax.broadcasted_iota(jnp.int32, (PB, PB), 0)
    col = lax.broadcasted_iota(jnp.int32, (PB, PB), 1)
    lower = work[...]
    top = jnp.where(row >= col, lower, lower.T)
    work[...] = kern + jnp.where(row == col, JITTER, 0.0) + top * over
    t, logs = inverse_of(work[:128, :128], piece)
    rest = jnp.dot(t, work[:128, 128:], preferred_element_type=F32, precision=HI)
    u = jnp.concatenate([t, rest], axis=1)
    inverse_ref[...] = jnp.where(lax.broadcasted_iota(jnp.int32, (128, PB), 1) < 128, u, 0.0)
    away = lax.dot_general(rest, u, TN, preferred_element_type=F32, precision=HI)
    column = lax.broadcasted_iota(jnp.int32, (PB - 128, PB), 1)
    left_ref[...] = jnp.where(column < 128, 0.0, work[128:, :]) - away
    log_ref[...] = jnp.sum(logs[:1, :], axis=1, keepdims=True)


def factor_middle_kernel(work_ref, inverse_ref, log_ref, left_ref, piece):
    t, logs = inverse_of(work_ref[:128, 128:256], piece)
    rest = jnp.dot(t, work_ref[:128, :], preferred_element_type=F32, precision=HI)
    u = jnp.concatenate([rest[:, :128], t, rest[:, 256:]], axis=1)
    inverse_ref[...] = jnp.where(lax.broadcasted_iota(jnp.int32, (128, PB), 1) < 256, u, 0.0)
    away = lax.dot_general(u[:, 256:], u, TN, preferred_element_type=F32, precision=HI)
    column = lax.broadcasted_iota(jnp.int32, (PB - 256, PB), 1)
    left_ref[...] = jnp.where((column >= 128) & (column < 256), 0.0, work_ref[128:, :]) - away
    log_ref[...] = jnp.sum(logs[:1, :], axis=1, keepdims=True)


def factor_last_kernel(work_ref, inverse_ref, log_ref, work, across_ref, piece):
    done = PB - work.shape[0]
    work[...] = work_ref[...]
    row = done + lax.broadcasted_iota(jnp.int32, work.shape, 0)
    column = lax.broadcasted_iota(jnp.int32, work.shape, 1)

    def one(k, total):
        lo = pl.multiple_of(128 * k, 128)
        rows = pl.ds(pl.multiple_of(128 * k - done, 128), 128)
        t, logs = inverse_of(work[rows, pl.ds(lo, 128)], piece)
        across_ref[...] = jnp.dot(t, work[rows, :], preferred_element_type=F32, precision=HI)
        across_ref[:, pl.ds(lo, 128)] = t
        u = across_ref[...]
        inverse_ref[rows, :] = jnp.where(column[:128] < lo + 128, u, 0.0)
        away = lax.dot_general(u[:, done:], u, TN, preferred_element_type=F32, precision=HI)
        inside = (column >= lo) & (column < lo + 128)
        left = jnp.where(inside, 0.0, work[...]) - away
        work[...] = jnp.where(row >= lo + 128, left, work[...])
        return total + logs

    total = lax.fori_loop(done // 128, PB // 128, one, jnp.zeros((8, 128), F32))
    log_ref[...] = jnp.sum(total[:1, :], axis=1, keepdims=True)


def factor_first(ids, log_scale, lengthscale, noise_var, panel, mine, other):
    full = pl.BlockSpec(memory_space=pltpu.VMEM)
    smem = pl.BlockSpec(memory_space=pltpu.SMEM)
    return pl.pallas_call(
        factor_first_kernel,
        out_shape=(
            jax.ShapeDtypeStruct((128, PB), F32),
            jax.ShapeDtypeStruct((1, 1), F32),
            jax.ShapeDtypeStruct((PB - 128, PB), F32),
            jax.ShapeDtypeStruct((1, PB), F32),
        ),
        in_specs=[smem] + [full] * 6,
        out_specs=(full,) * 4,
        scratch_shapes=[pltpu.VMEM((PB, PB), F32), pltpu.VMEM((128, 128), F32)],
        compiler_params=vmem(20 << 20),
        cost_estimate=pl.CostEstimate(flops=6 * 10**9, bytes_accessed=2 << 20, transcendentals=1 << 18),
        name="factor_first",
    )(ids, log_scale, lengthscale, noise_var, panel, mine, other)


def factor_middle(work):
    full = pl.BlockSpec(memory_space=pltpu.VMEM)
    return pl.pallas_call(
        factor_middle_kernel,
        out_shape=(
            jax.ShapeDtypeStruct((128, PB), F32),
            jax.ShapeDtypeStruct((1, 1), F32),
            jax.ShapeDtypeStruct((PB - 256, PB), F32),
        ),
        in_specs=[full],
        out_specs=(full,) * 3,
        scratch_shapes=[pltpu.VMEM((128, 128), F32)],
        compiler_params=vmem(20 << 20),
        cost_estimate=pl.CostEstimate(flops=5 * 10**9, bytes_accessed=2 << 20, transcendentals=1 << 18),
        name="factor_middle",
    )(work)


def factor_last(work):
    full = pl.BlockSpec(memory_space=pltpu.VMEM)
    return pl.pallas_call(
        factor_last_kernel,
        out_shape=(jax.ShapeDtypeStruct(work.shape, F32), jax.ShapeDtypeStruct((1, 1), F32)),
        in_specs=[full],
        out_specs=(full, full),
        scratch_shapes=[pltpu.VMEM(work.shape, F32), pltpu.VMEM((128, PB), F32), pltpu.VMEM((128, 128), F32)],
        compiler_params=vmem(20 << 20),
        cost_estimate=pl.CostEstimate(flops=10 * 10**9, bytes_accessed=2 << 20, transcendentals=1 << 18),
        name="factor_last",
    )(work)


def finish_kernel(ids_ref, log_ref, length_ref, noise_ref, own_ref, panel_ref, right_ref, *rest):
    inverse_refs, log_refs, parts = rest[:3], rest[3:6], rest[6:-4]
    pf_ref, rhs_ref, sol_ref, det_ref = rest[-4:]
    det_ref[...] = log_refs[0][...] + log_refs[1][...] + log_refs[2][...]
    i2, offset = scales(log_ref, length_ref)
    over = 1.0 / noise_ref[...]
    rows = own_ref.shape[0] // SHARDS
    own = own_ref[pl.ds(pl.multiple_of(ids_ref[32] * rows, rows), rows), :]
    left = widen(own, half_norm(own) + offset, True)
    right = widen(panel_ref[...], half_norm(panel_ref[...]), False)
    kern = jnp.exp2(i2 * lax.dot_general(left, right, NT, preferred_element_type=F32))
    row = ids_ref[34] + lax.broadcasted_iota(jnp.int32, (rows, PB), 0)
    col = lax.broadcasted_iota(jnp.int32, (rows, PB), 1)
    a, b, c, d = (p[...] for p in parts)
    sums = (a + b) + (c + d)
    system = kern + jnp.where(row == col, JITTER, 0.0) + sums[:rows, :] * over
    both = jnp.concatenate([system, jnp.broadcast_to(right_ref[...], (8, PB))], axis=0)
    inverse = jnp.concatenate([r[...] for r in inverse_refs], axis=0)
    solved = lax.dot_general(both, inverse, NT, preferred_element_type=F32, precision=HI)
    pf = solved[:rows, :]
    sol = solved[rows:, :]
    pf_ref[...] = pf
    sol_ref[...] = sol[:1, :]
    back = lax.dot_general(sol, pf, NT, preferred_element_type=F32, precision=HI)
    rhs_ref[...] = sums[rows : rows + 1, :rows] * over - back[:1, :]


def finish(ids, log_scale, lengthscale, noise_var, inducing, panel, *others):
    rows = inducing.shape[0] // SHARDS
    full = pl.BlockSpec(memory_space=pltpu.VMEM)
    return pl.pallas_call(
        finish_kernel,
        out_shape=(
            jax.ShapeDtypeStruct((rows, PB), F32),
            jax.ShapeDtypeStruct((1, rows), F32),
            jax.ShapeDtypeStruct((1, PB), F32),
            jax.ShapeDtypeStruct((1, 1), F32),
        ),
        in_specs=[pl.BlockSpec(memory_space=pltpu.SMEM)] + [full] * (5 + len(others)),
        out_specs=(full,) * 4,
        compiler_params=vmem(20 << 20),
        cost_estimate=pl.CostEstimate(flops=10**9, bytes_accessed=2 << 20, transcendentals=1 << 16),
        name="finish",
    )(ids, log_scale, lengthscale, noise_var, inducing, panel, *others)


def moved(x, axis, pairs):
    return lax.ppermute(x, axis, pairs)


def across(x, to):
    return lax.ppermute(x, "dp", [(i, to(i)) for i in range(SHARDS)])


def other_core(i):
    return i ^ 1


def along_x(i, k):
    return (i // 8) * 8 + (i + 2 * k) % 8


def along_y(i, k):
    return (i + 8 * k) % SHARDS


def gray(v):
    return v ^ (v >> 1)


def place_of(i):
    return i % 2, gray((i // 2) % 4), gray(i // 8)


def device_at(c, gx, gy):
    return gray(gy) * 8 + gray(gx) * 2 + c


def flipped(i, bit, which):
    c, gx, gy = place_of(i)
    return device_at(c, gx ^ (bit * (which >> 1)), gy ^ (bit * (which & 1)))


def device_numbers(shard, layer, row):
    n = jnp.arange(40, dtype=jnp.int32)
    r = n & 31
    c, gx, gy = place_of(shard)
    gx = gx ^ (((r >> 3) & 1) | (((r >> 1) & 1) << 1))
    gy = gy ^ (((r >> 2) & 1) | ((r & 1) << 1))
    order = device_at(c ^ (r >> 4), gx, gy)
    return jnp.where(n < 32, order, jnp.where(n == 32, shard, jnp.where(n == 33, layer, row))).astype(jnp.int32)


def quarters(*parts):
    n = parts[0].shape[0] // 4
    return [sum(p[n * w : n * w + n] for p in parts) for w in range(4)]


def spread_blocks(sent, bit):
    return [sent[0]] + [
        across(sent[w], functools.partial(flipped, bit=bit, which=w)) for w in (3, 2, 1)
    ]


def after(x, *first):
    return lax.optimization_barrier((x,) + first)[0]


def sum_over(x, step):
    a, b, c = (across(x, functools.partial(step, k=k)) for k in (1, 2, 3))
    return (x + a) + (b + c)


def every_share(half):
    ring = lambda k: moved(half, "ind", [(i, (i - k) % LAYERS) for i in range(LAYERS)])
    shares = [half, ring(1), ring(2), ring(-1)]
    return jnp.stack(shares)


def body(
    inputs, targets, row_counts, w_in, w_mid, w_out, feat_gain, inducing, log_scale, lengthscale, noise_var
):
    shard = lax.axis_index("dp").astype(jnp.int32)
    layer = lax.axis_index("ind").astype(jnp.int32)
    slots = inputs.shape[0]
    own_rows = inducing.shape[0] // SHARDS
    ids = device_numbers(shard, layer, layer * inducing.shape[0] + shard * own_rows)
    shape = (log_scale.reshape(1, 1), lengthscale.reshape(1, 1))
    noise = noise_var.reshape(1, 1)
    trow = targets.astype(F32).reshape(1, slots)
    network = (w_in, w_mid, w_out, feat_gain.reshape(1, -1))

    panel = inducing[:PB]
    far = [moved(panel, "ind", [(0, 3)]), moved(panel, "ind", [(0, 5)])]
    samples = embed(0, 2, ids, row_counts, inputs, *network)
    panel = jnp.where(layer == 3, far[0], jnp.where(layer == 5, far[1], panel))
    panel = after(panel, samples)
    near = [
        moved(panel, "ind", [(0, 1), (3, 4), (5, 6)]),
        moved(panel, "ind", [(0, 7), (3, 2)]),
    ]
    samples = embed(2, 2, ids, row_counts, after(inputs, panel), *network, before=samples)
    in_first = (layer == 1) | (layer == 4) | (layer == 6)
    in_second = (layer == 7) | (layer == 2)
    panel = jnp.where(in_first, near[0], jnp.where(in_second, near[1], panel))

    pt, half, sent = panel_top(ids, *shape, samples, panel, trow)
    half = half + across(sent, other_core)
    away = gram(ids, 16, 16, *shape, inducing, samples, pt, trow)
    got = across(after(away, half), other_core)
    half = after(half, away)
    half = sum_over(half, along_x)
    kept = gram(ids, 0, 16, *shape, inducing, samples, pt, trow)
    half = sum_over(half, along_y)
    sums = quarters(kept, got)
    parts = spread_blocks(sums, 1)
    mine = every_share(half)
    other = across(mine, other_core)
    inverse0, log0, work, right = factor_first(ids, *shape, noise, panel, mine, other)
    inverse1, log1, work = factor_middle(work)
    parts = spread_blocks(quarters(after(parts[0], work), *parts[1:]), 2)
    inverse2, log2 = factor_last(work)
    pf, rhs, sol, det = finish(
        ids, *shape, noise, inducing, panel, right, inverse0, inverse1, inverse2, log0, log1, log2, *(p[0] for p in parts)
    )
    return pf, rhs.reshape(own_rows), sol.reshape(PB), det.reshape(1)


def solution(mesh):
    return jax.shard_map(
        body,
        mesh=mesh,
        in_specs=(P("dp", None), P("dp"), P(), P(), P(), P(), P(), P("ind", None), P(), P(), P()),
        out_specs=(P(("ind", "dp"), None), P(("ind", "dp")), P(), P()),
        check_vma=False,
    )
```
